1024 devices in a mesh: wide: 32 (over y, x, core), narrow: 32 (over z).
Axes of the slice: x: 4, y: 4, z: 32, core: 2. Of those that a mesh axis runs over, the one named last changes fastest.
Arguments:
- volumes: bfloat16 [32, 1, 4, 128, 4096], P('narrow', None, None, 'wide'), may hold values from -6 to 6
- first_kernel: bfloat16 [27, 32, 4], replicated, may hold values from -0.625 to 0.625
- second_kernel: bfloat16 [27, 64, 32], replicated, may hold values from -0.21875 to 0.21875
- cotangent: bfloat16 [32, 1, 64, 65536], P('narrow', None, None, 'wide'), may hold values from -6 to 6
Outputs:
- activations: bfloat16 [32, 1, 64, 65536], P('narrow', None, None, 'wide')
- weight_grad: float32 [27, 64, 32], P(None, 'narrow')
The draws below stay inside these ranges and needn't reach their ends.
All inputs are finite; a program needn't handle non-finite values.
Results may differ from the reference program's by a relative error of at most 0.023.
The reference program's roundings to bfloat16 on the way (of `first_act` and `back`) count: a program that leaves them out, or rounds other values in their place, can miss the bound.
Values may be sent and summed in bfloat16 or wider, within the bound.
A program may use at most 32 MiB of HBM per device.

```python
import math
import jax
import jax.numpy as jnp
from jax import lax

CIN = 4
C1 = 32
C2 = 64
SAMP = 1
YCELLS = 64
XCELLS = 64
NZ = 128
GROUPS = 32


def shard_levels(stream_key, shape, split, least, largest):
    loudness = 1.0
    for dim, parts in split:
        heights = jax.random.uniform(jax.random.fold_in(jax.random.fold_in(stream_key, 6), dim), (parts,), jnp.float32, least / len(split), largest / len(split))
        loudness = loudness * jnp.repeat(jnp.exp(heights), shape[dim] // parts).reshape((-1,) + (1,) * (len(shape) - 1 - dim))
    return loudness


def gaussian(stream_key, dims, deviation, reach, split=(), kind=jnp.bfloat16):
    result = deviation * jax.random.normal(stream_key, dims, jnp.float32)
    if split:
        result = result * shard_levels(stream_key, dims, split, -0.22, 0.18)
    return jnp.clip(result, -reach, reach).astype(kind)


def setup_inputs(seed: int = 0) -> dict:
    splits = jax.random.split(jax.random.key(seed), 5)
    volumes = gaussian(splits[0], (GROUPS, SAMP, CIN, NZ, YCELLS * XCELLS), 1.0, 6.0, ((0, 32), (3, 32)))
    first_kernel = gaussian(splits[1], (27, C1, CIN), (27 * CIN) ** -0.5, 0.625)
    second_kernel = gaussian(splits[2], (27, C2, C1), (27 * C1) ** -0.5, 0.21875)
    cotangent = gaussian(splits[3], (GROUPS, SAMP, C2, (NZ // 2) * (YCELLS // 2) * (XCELLS // 2)), 1.0, 6.0, ((0, 32), (3, 32)))
    return dict(volumes=volumes, first_kernel=first_kernel, second_kernel=second_kernel, cotangent=cotangent)


neg_slope = 0.3

def leaky_relu(value):
    return jnp.where(value > 0, value, neg_slope * value)

def kernel_layout(kernel):
    outs_n = kernel.shape[1]
    ins_n = kernel.shape[2]
    return kernel.reshape(3, 3, 3, outs_n, ins_n).transpose(3, 4, 0, 1, 2)

def convolve(inputs, kernel, stride, padding, precision):
    return lax.conv_general_dilated(inputs, kernel_layout(kernel), (stride, stride, stride), [padding, padding, padding], dimension_numbers=('NCDHW', 'OIDHW', 'NCDHW'), precision=precision, preferred_element_type=jnp.float32)

def reference(volumes, first_kernel, second_kernel, cotangent):
    samples = volumes.reshape(-1, CIN, NZ, YCELLS, XCELLS)
    cells_out = NZ // 2 * (YCELLS // 2) * (XCELLS // 2)
    cot_flat = cotangent.reshape(-1, C2, cells_out)

    def one_sample(grads, inputs):
        sample, cot = inputs
        first_pre = convolve(sample[None], first_kernel, 2, (1, 0), None)
        first_act = leaky_relu(first_pre).astype(jnp.bfloat16)
        second_pre = convolve(first_act, second_kernel, 1, (1, 1), None)
        pre = second_pre.reshape(C2, cells_out)
        output = leaky_relu(pre).astype(jnp.bfloat16)
        back = (cot.astype(jnp.float32) * jnp.where(pre > 0, 1.0, neg_slope)).astype(jnp.bfloat16)
        act_wide = first_act.astype(jnp.float32)

        def apply_kernel(kernel):
            return convolve(act_wide, kernel, 1, (1, 1), lax.Precision.HIGHEST)
        primal, pullback = jax.vjp(apply_kernel, second_kernel.astype(jnp.float32))
        back_grid = back.astype(jnp.float32).reshape(primal.shape)
        term = pullback(back_grid)[0]
        return (grads + term, output)
    start = jnp.zeros((27, C2, C1), jnp.float32)
    grads, outputs = lax.scan(one_sample, start, (samples, cot_flat))
    count = GROUPS * SAMP * cells_out
    weight_grad = grads * (1.0 / math.sqrt(count))
    return (outputs.reshape(GROUPS, SAMP, C2, cells_out), weight_grad)
```

```python
import functools
import math

import jax
import jax.numpy as jnp
import numpy as np
from jax import lax
from jax.experimental import pallas as pl
from jax.experimental.pallas import tpu as pltpu
from jax.sharding import PartitionSpec as P

CIN = 4
C1 = 32
C2 = 64
HALF = 32
PLANE = HALF * HALF
SLOPE = 0.3
TAPS = 27
WIDTH = 896
ROWS2 = 9 * C1
F32 = jnp.float32
BF16 = jnp.bfloat16
MESH = pl.DeviceIdType.MESH


def lane_order():
    order = np.zeros((512, 512), np.float32)
    for k in range(4):
        for py in range(2):
            for x in range(64):
                order[k * 128 + py * 64 + x, (py * 2 + x % 2) * 128 + k * 32 + x // 2] = 1.0
    return order


def row_order():
    order = np.zeros((64, 64), np.float32)
    for z in range(4):
        for q in range(4):
            for ch in range(CIN):
                order[z * 16 + q * 4 + ch, q * 16 + ch * 4 + z] = 1.0
    return order


def first_places():
    places = np.zeros((TAPS, CIN, 256), np.float32)
    for t in range(TAPS):
        a, b, c = t // 9, t // 3 % 3, t % 3
        shift = (2 if b == 0 else 0) + (1 if c == 0 else 0)
        q = (0 if b == 1 else 2) + (0 if c == 1 else 1)
        for i in range(CIN):
            places[t, i, a * 64 + shift * 16 + q * 4 + i] = 1.0
    return places


def rolled(x, shift):
    return pltpu.roll(x, shift % PLANE, axis=1)


def kernel(
    n, scale, vol_ref, k1_ref, k2_ref, cot_ref, lanes_ref, rows_ref, places_ref,
    act_ref, grad_ref,
    raw, planes, taps1, taps2, weights2, spread, send1, recv1, send2, recv2, send3, final,
    halo_send, halo_recv, sem_send1, sem_recv1, sem_send2, sem_recv2, sem_send3, sem_recv3, ready,
):
    w = lax.axis_index("wide")
    z = lax.axis_index("narrow")
    gap = lax.rem(z - w + n, n)
    steps = jnp.minimum(gap, n - gap)
    owner = gap == 0
    above = lax.rem(z + 1, n)
    below = lax.rem(z + n - 1, n)
    barrier = pltpu.get_barrier_semaphore()

    def greet(k, carry):
        pl.semaphore_signal(barrier, 1, device_id={"wide": lax.rem(w + k, n)}, device_id_type=MESH)
        return carry

    lax.fori_loop(1, n, greet, 0)
    pl.semaphore_signal(barrier, 1, device_id={"narrow": above}, device_id_type=MESH)
    pl.semaphore_signal(barrier, 1, device_id={"narrow": below}, device_id_type=MESH)

    def announce(up, down):
        @pl.when(up)
        def _():
            pl.semaphore_signal(ready, 1, device_id={"narrow": above}, device_id_type=MESH)

        @pl.when(down)
        def _():
            pl.semaphore_signal(ready, 1, device_id={"narrow": below}, device_id_type=MESH)

    def relay(least, most):
        @pl.when((steps >= least) & (steps <= most))
        def _():
            pl.semaphore_wait(ready, 1)
            announce(gap < n // 2, gap > n // 2 + 1)

    for ch in range(CIN):
        raw[4 * ch : 4 * ch + 4, :] = vol_ref[ch].astype(F32)
    blocks = [raw[:, 512 * j : 512 * j + 512].astype(BF16) for j in range(8)]
    spreadout = jnp.dot(jnp.concatenate(blocks, axis=0), lanes_ref[...], preferred_element_type=F32).astype(BF16)
    joined = jnp.concatenate(
        [
            jnp.concatenate([spreadout[16 * j : 16 * j + 16, 128 * q : 128 * q + 128] for j in range(8)], axis=1)
            for q in range(4)
        ],
        axis=0,
    )
    planes[48:112, :] = jnp.dot(rows_ref[...], joined, preferred_element_type=F32).astype(BF16)

    first = w == 0
    last = w == n - 1

    @pl.when(first)
    def _():
        planes[0:48, :] = jnp.zeros((48, PLANE), BF16)

    @pl.when(last)
    def _():
        planes[112:144, :] = jnp.zeros((32, PLANE), BF16)

    pl.semaphore_wait(barrier, n + 1)

    upward = pltpu.make_async_remote_copy(
        planes.at[64:112], planes.at[0:48], halo_send.at[0], halo_recv.at[0],
        device_id={"wide": lax.rem(w + 1, n)}, device_id_type=MESH,
    )
    downward = pltpu.make_async_remote_copy(
        planes.at[48:80], planes.at[112:144], halo_send.at[1], halo_recv.at[1],
        device_id={"wide": lax.rem(w + n - 1, n)}, device_id_type=MESH,
    )

    @pl.when(jnp.logical_not(last))
    def _():
        upward.start()

    @pl.when(jnp.logical_not(first))
    def _():
        downward.start()

    @pl.when(owner)
    def _():
        announce(n > 1, n > 2)

    weights1 = jnp.zeros((C1, 256), F32)
    for t in range(TAPS):
        weights1 = weights1 + jnp.dot(k1_ref[t], places_ref[t], preferred_element_type=F32)
    weights1 = weights1[:, :192].astype(BF16)
    for k in range(7):
        pieces = [k2_ref[4 * k + r] if 4 * k + r < TAPS else jnp.zeros((C2, C1), BF16) for r in range(4)]
        weights2[:, 128 * k : 128 * k + 128] = jnp.concatenate(pieces, axis=1)

    lane = lax.broadcasted_iota(jnp.int32, (16, PLANE), 1)
    left_ok = (lane % HALF) != 0
    lower_ok = lane >= HALF

    def spread_plane(zi):
        base = planes[16 * zi : 16 * zi + 16, :].astype(F32)
        at_x = jnp.where(left_ok, rolled(base, 1), 0.0)
        at_y = jnp.where(lower_ok, rolled(base, HALF), 0.0)
        both = jnp.where(lower_ok, rolled(at_x, HALF), 0.0)
        for s, part in enumerate((base, at_x, at_y, both)):
            taps1[64 * zi + 16 * s : 64 * zi + 16 * s + 16, :] = part.astype(BF16)

    for zi in range(3, 7):
        spread_plane(zi)
    taps2[4 * ROWS2 :, :] = jnp.zeros((32, PLANE), BF16)

    @pl.when(jnp.logical_not(last))
    def _():
        upward.wait_send()
        downward.wait_recv()

    @pl.when(jnp.logical_not(first))
    def _():
        downward.wait_send()
        upward.wait_recv()

    relay(1, 4)

    for zi in (0, 1, 2, 7, 8):
        spread_plane(zi)

    lane2 = lax.broadcasted_iota(jnp.int32, (C1, PLANE), 1)
    left2 = (lane2 % HALF) != 0
    right2 = (lane2 % HALF) != HALF - 1
    lower2 = lane2 >= HALF
    upper2 = lane2 < PLANE - HALF

    for zo in range(4):
        pre = jnp.dot(weights1, taps1[128 * zo : 128 * zo + 192, :], preferred_element_type=F32)
        act = jnp.where(pre > 0, pre, SLOPE * pre)
        if zo == 3:
            act = jnp.where(last, 0.0, act)
        act = act.astype(BF16).astype(F32)
        across = (jnp.where(left2, rolled(act, 1), 0.0), act, jnp.where(right2, rolled(act, -1), 0.0))
        for c in range(3):
            parts = (
                jnp.where(lower2, rolled(across[c], HALF), 0.0),
                across[c],
                jnp.where(upper2, rolled(across[c], -HALF), 0.0),
            )
            for b in range(3):
                row = ROWS2 * zo + C1 * (3 * b + c)
                taps2[row : row + C1, :] = parts[b].astype(BF16)
        relay(5 + 2 * zo, 6 + 2 * zo)

    total = None
    for half in range(2):
        patches = taps2[ROWS2 * half : ROWS2 * half + WIDTH, :]
        pre = jnp.dot(weights2[...], patches, preferred_element_type=F32)
        cells = slice(PLANE * half, PLANE * half + PLANE)
        act_ref[:, cells] = jnp.where(pre > 0, pre, SLOPE * pre).astype(BF16)
        back = (cot_ref[:, cells].astype(F32) * jnp.where(pre > 0, 1.0, SLOPE)).astype(BF16)
        term = lax.dot_general(back, patches, (((1,), (1,)), ((), ())), preferred_element_type=F32)
        total = term if total is None else total + term
        relay(13 + 2 * half, 14 + 2 * half)
    relay(17, n)

    total = total * scale
    for k in range(7):
        spread[pl.ds(k, C2, stride=8), :] = total[:, 128 * k : 128 * k + 128]
    spread[pl.ds(7, C2, stride=8), :] = jnp.zeros((C2, 128), F32)
    size = C2 // n * 8
    send1[...] = spread[...].astype(BF16).reshape(n, size, 128)
    recv1[w] = send1[w]

    def scatter(k, carry):
        to = lax.rem(w + k, n)
        pltpu.make_async_remote_copy(
            send1.at[to], recv1.at[w], sem_send1, sem_recv1, device_id={"wide": to}, device_id_type=MESH
        ).start()
        return carry

    lax.fori_loop(1, n, scatter, 0)
    pltpu.make_async_copy(send1.at[pl.ds(0, n - 1)], send1.at[pl.ds(0, n - 1)], sem_send1).wait()
    pltpu.make_async_copy(recv1.at[pl.ds(0, n - 1)], recv1.at[pl.ds(0, n - 1)], sem_recv1).wait()

    send2[...] = jnp.sum(recv1[...].astype(F32), axis=0)

    deliver = pltpu.make_async_remote_copy(
        send2, recv2.at[z], sem_send2, sem_recv2, device_id={"narrow": w}, device_id_type=MESH
    )

    @pl.when(jnp.logical_not(owner))
    def _():
        deliver.start()
        deliver.wait_send()
        pltpu.make_async_copy(final, final, sem_recv3).wait()

    @pl.when(owner)
    def _():
        recv2[z] = send2[...]
        pltpu.make_async_copy(recv2.at[pl.ds(0, n - 1)], recv2.at[pl.ds(0, n - 1)], sem_recv2).wait()
        whole = jnp.sum(recv2[...], axis=0)
        send3[...] = whole
        final[...] = whole

        def hand_out(k, carry):
            pltpu.make_async_remote_copy(
                send3, final, sem_send3, sem_recv3, device_id={"wide": lax.rem(w + k, n)}, device_id_type=MESH
            ).start()
            return carry

        lax.fori_loop(1, n, hand_out, 0)
        pltpu.make_async_copy(recv2.at[pl.ds(0, n - 1)], recv2.at[pl.ds(0, n - 1)], sem_send3).wait()

    rows = C2 // n
    for t in range(TAPS):
        for r in range(rows):
            at = 8 * r + t // 4
            grad_ref[t, r : r + 1, :] = final[at : at + 1, C1 * (t % 4) : C1 * (t % 4) + C1]


def body(volumes, first_kernel, second_kernel, cotangent):
    n = lax.axis_size("wide")
    cells = cotangent.shape[3]
    scale = 1.0 / math.sqrt(n * lax.axis_size("narrow") * cells)
    size = C2 // n * 8
    vmem = pl.BlockSpec(memory_space=pltpu.VMEM)
    dma = pltpu.SemaphoreType.DMA
    act, grad = pl.pallas_call(
        functools.partial(kernel, n, scale),
        out_shape=(
            jax.ShapeDtypeStruct((C2, cells), BF16),
            jax.ShapeDtypeStruct((TAPS, C2 // n, C1), F32),
        ),
        in_specs=[vmem] * 7,
        out_specs=(vmem, vmem),
        scratch_shapes=[
            pltpu.VMEM((16, 4096), F32),
            pltpu.VMEM((144, PLANE), BF16),
            pltpu.VMEM((576, PLANE), BF16),
            pltpu.VMEM((4 * ROWS2 + 32, PLANE), BF16),
            pltpu.VMEM((C2, WIDTH), BF16),
            pltpu.VMEM((C2 * 8, 128), F32),
            pltpu.VMEM((n, size, 128), BF16),
            pltpu.VMEM((n, size, 128), BF16),
            pltpu.VMEM((size, 128), F32),
            pltpu.VMEM((n, size, 128), F32),
            pltpu.VMEM((size, 128), F32),
            pltpu.VMEM((size, 128), F32),
            dma((2,)),
            dma((2,)),
            dma(()),
            dma(()),
            dma(()),
            dma(()),
            dma(()),
            dma(()),
            pltpu.SemaphoreType.REGULAR,
        ],
        compiler_params=pltpu.CompilerParams(collective_id=0, has_side_effects=True),
    )(
        volumes.reshape(CIN, 4, 4096),
        first_kernel,
        second_kernel,
        cotangent.reshape(C2, cells),
        jnp.asarray(lane_order(), BF16),
        jnp.asarray(row_order(), BF16),
        jnp.asarray(first_places(), BF16),
    )
    return act.reshape(1, 1, C2, cells), grad


def solution(mesh):
    return jax.shard_map(
        body,
        mesh=mesh,
        in_specs=(P("narrow", None, None, "wide", None), P(), P(), P("narrow", None, None, "wide")),
        out_specs=(P("narrow", None, None, "wide"), P(None, "narrow", None)),
        check_vma=False,
    )
```

```python
import functools
import math

import jax
import jax.numpy as jnp
import numpy as np
from jax import lax
from jax.experimental import pallas as pl
from jax.experimental.pallas import tpu as pltpu
from jax.sharding import PartitionSpec as P

CIN = 4
C1 = 32
C2 = 64
HALF = 32
PLANE = HALF * HALF
SLOPE = 0.3
TAPS = 27
WIDTH = 896
ROWS2 = 9 * C1
F32 = jnp.float32
BF16 = jnp.bfloat16
MESH = pl.DeviceIdType.MESH


def lane_order():
    order = np.zeros((512, 512), np.float32)
    for k in range(4):
        for py in range(2):
            for x in range(64):
                order[k * 128 + py * 64 + x, (py * 2 + x % 2) * 128 + k * 32 + x // 2] = 1.0
    return order


def row_order():
    order = np.zeros((64, 64), np.float32)
    for z in range(4):
        for q in range(4):
            for ch in range(CIN):
                order[z * 16 + q * 4 + ch, q * 16 + ch * 4 + z] = 1.0
    return order


def first_places():
    places = np.zeros((256, 128), np.float32)
    for t in range(TAPS):
        a, b, c = t // 9, t // 3 % 3, t % 3
        shift = (2 if b == 0 else 0) + (1 if c == 0 else 0)
        q = (0 if b == 1 else 2) + (0 if c == 1 else 1)
        for i in range(CIN):
            places[a * 64 + shift * 16 + q * 4 + i, CIN * t + i] = 1.0
    return places


def rolled(x, shift):
    return pltpu.roll(x, shift % PLANE, axis=1)


def turned(x, size):
    rows = lax.broadcasted_iota(jnp.int32, (size, size), 0)
    columns = lax.broadcasted_iota(jnp.int32, (size, size), 1)
    same = jnp.where(rows == columns, 1.0, 0.0).astype(BF16)
    return lax.dot_general(same, x, (((1,), (1,)), ((), ())), preferred_element_type=F32).astype(BF16)


def kernel(
    n, scale, vol_hbm, lanes_hbm, rows_hbm, places_hbm, k1_hbm, k2_hbm, cot_hbm,
    act_ref, grad_ref,
    vol_ref, lanes_ref, rows_ref, places_ref, k1_ref, k2_ref, cot_ref, loads,
    raw, stacked, planes, taps1, taps2, weights2, spread, send1, recv1, send2, recv2, send3, final,
    halo_send, halo_recv, sem_send1, sem_recv1, sem_send2, sem_recv2, sem_send3, sem_recv3, ready,
):
    w = lax.axis_index("wide")
    z = lax.axis_index("narrow")
    gap = lax.rem(z - w + n, n)
    owner = gap == 0
    above = lax.rem(z + 1, n)
    below = lax.rem(z + n - 1, n)
    barrier = pltpu.get_barrier_semaphore()

    def greet(k, carry):
        pl.semaphore_signal(barrier, 1, device_id={"wide": lax.rem(w + k, n)}, device_id_type=MESH)
        return carry

    lax.fori_loop(1, n, greet, 0)
    pl.semaphore_signal(barrier, 1, device_id={"narrow": above}, device_id_type=MESH)
    pl.semaphore_signal(barrier, 1, device_id={"narrow": below}, device_id_type=MESH)

    def announce(up, down):
        @pl.when(up)
        def _():
            pl.semaphore_signal(ready, 1, device_id={"narrow": above}, device_id_type=MESH)

        @pl.when(down)
        def _():
            pl.semaphore_signal(ready, 1, device_id={"narrow": below}, device_id_type=MESH)

    def relay():
        @pl.when(jnp.logical_not(owner))
        def _():
            pl.semaphore_wait(ready, 1)
            announce(gap < n // 2, gap > n // 2 + 1)

    pairs = (
        (vol_hbm, vol_ref), (lanes_hbm, lanes_ref), (rows_hbm, rows_ref), (places_hbm, places_ref),
        (k1_hbm, k1_ref), (k2_hbm, k2_ref), (cot_hbm, cot_ref),
    )
    copies = [pltpu.make_async_copy(source, target, loads.at[i]) for i, (source, target) in enumerate(pairs)]
    for copy in copies:
        copy.start()

    for copy in copies[:3]:
        copy.wait()
    for ch in range(CIN):
        raw[4 * ch : 4 * ch + 4, :] = vol_ref[ch].astype(F32)
    blocks = [raw[:, 512 * j : 512 * j + 512].astype(BF16) for j in range(8)]
    spreadout = jnp.dot(jnp.concatenate(blocks, axis=0), lanes_ref[...], preferred_element_type=F32).astype(BF16)
    joined = jnp.concatenate(
        [
            jnp.concatenate([spreadout[16 * j : 16 * j + 16, 128 * q : 128 * q + 128] for j in range(8)], axis=1)
            for q in range(4)
        ],
        axis=0,
    )
    planes[48:112, :] = jnp.dot(rows_ref[...], joined, preferred_element_type=F32).astype(BF16)

    first = w == 0
    last = w == n - 1

    @pl.when(first)
    def _():
        planes[0:48, :] = jnp.zeros((48, PLANE), BF16)

    @pl.when(last)
    def _():
        planes[112:144, :] = jnp.zeros((32, PLANE), BF16)

    pl.semaphore_wait(barrier, n + 1)

    upward = pltpu.make_async_remote_copy(
        planes.at[64:112], planes.at[0:48], halo_send.at[0], halo_recv.at[0],
        device_id={"wide": lax.rem(w + 1, n)}, device_id_type=MESH,
    )
    downward = pltpu.make_async_remote_copy(
        planes.at[48:80], planes.at[112:144], halo_send.at[1], halo_recv.at[1],
        device_id={"wide": lax.rem(w + n - 1, n)}, device_id_type=MESH,
    )

    @pl.when(jnp.logical_not(last))
    def _():
        upward.start()

    @pl.when(jnp.logical_not(first))
    def _():
        downward.start()

    @pl.when(owner)
    def _():
        announce(n > 1, n > 2)

    for copy in copies[3:]:
        copy.wait()
    for t in range(TAPS):
        stacked[CIN * t : CIN * t + CIN, :] = k1_ref[t].astype(F32)
    stacked[CIN * TAPS :, :] = jnp.zeros((128 - CIN * TAPS, C1), F32)
    placed = jnp.dot(places_ref[...], stacked[...].astype(BF16), preferred_element_type=F32).astype(BF16)
    weights1 = turned(placed, C1)[:, :192]
    weights2[:, : TAPS * C1] = turned(k2_ref[...].reshape(TAPS * C1, C2), C2)
    weights2[:, TAPS * C1 :] = jnp.zeros((C2, WIDTH - TAPS * C1), BF16)

    lane = lax.broadcasted_iota(jnp.int32, (16, PLANE), 1)
    left_ok = (lane % HALF) != 0
    lower_ok = lane >= HALF

    def spread_plane(zi):
        base = planes[16 * zi : 16 * zi + 16, :].astype(F32)
        at_x = jnp.where(left_ok, rolled(base, 1), 0.0)
        at_y = jnp.where(lower_ok, rolled(base, HALF), 0.0)
        both = jnp.where(lower_ok, rolled(at_x, HALF), 0.0)
        for s, part in enumerate((base, at_x, at_y, both)):
            taps1[64 * zi + 16 * s : 64 * zi + 16 * s + 16, :] = part.astype(BF16)

    for zi in range(3, 7):
        spread_plane(zi)
    taps2[4 * ROWS2 :, :] = jnp.zeros((32, PLANE), BF16)

    @pl.when(jnp.logical_not(last))
    def _():
        upward.wait_send()
        downward.wait_recv()

    @pl.when(jnp.logical_not(first))
    def _():
        downward.wait_send()
        upward.wait_recv()

    for zi in (0, 1, 2, 7, 8):
        spread_plane(zi)

    lane2 = lax.broadcasted_iota(jnp.int32, (C1, PLANE), 1)
    left2 = (lane2 % HALF) != 0
    right2 = (lane2 % HALF) != HALF - 1
    lower2 = lane2 >= HALF
    upper2 = lane2 < PLANE - HALF

    for zo in range(4):
        pre = jnp.dot(weights1, taps1[128 * zo : 128 * zo + 192, :], preferred_element_type=F32)
        act = jnp.where(pre > 0, pre, SLOPE * pre)
        if zo == 3:
            act = jnp.where(last, 0.0, act)
        act = act.astype(BF16).astype(F32)
        across = (jnp.where(left2, rolled(act, 1), 0.0), act, jnp.where(right2, rolled(act, -1), 0.0))
        for c in range(3):
            parts = (
                jnp.where(lower2, rolled(across[c], HALF), 0.0),
                across[c],
                jnp.where(upper2, rolled(across[c], -HALF), 0.0),
            )
            for b in range(3):
                row = ROWS2 * zo + C1 * (3 * b + c)
                taps2[row : row + C1, :] = parts[b].astype(BF16)

    total = None
    for half in range(2):
        patches = taps2[ROWS2 * half : ROWS2 * half + WIDTH, :]
        pre = jnp.dot(weights2[...], patches, preferred_element_type=F32)
        cells = slice(PLANE * half, PLANE * half + PLANE)
        act_ref[:, cells] = jnp.where(pre > 0, pre, SLOPE * pre).astype(BF16)
        back = (cot_ref[:, cells].astype(F32) * jnp.where(pre > 0, 1.0, SLOPE)).astype(BF16)
        term = lax.dot_general(back, patches, (((1,), (1,)), ((), ())), preferred_element_type=F32)
        total = term if total is None else total + term

    total = total * scale
    for k in range(7):
        spread[pl.ds(k, C2, stride=8), :] = total[:, 128 * k : 128 * k + 128]
    spread[pl.ds(7, C2, stride=8), :] = jnp.zeros((C2, 128), F32)
    size = C2 // n * 8
    send1[...] = spread[...].astype(BF16).reshape(n, size, 128)
    recv1[w] = send1[w]

    def scatter(k, carry):
        to = lax.rem(w + k, n)
        pltpu.make_async_remote_copy(
            send1.at[to], recv1.at[w], sem_send1, sem_recv1, device_id={"wide": to}, device_id_type=MESH
        ).start()
        return carry

    lax.fori_loop(1, n, scatter, 0)
    relay()
    pltpu.make_async_copy(send1.at[pl.ds(0, n - 1)], send1.at[pl.ds(0, n - 1)], sem_send1).wait()
    pltpu.make_async_copy(recv1.at[pl.ds(0, n - 1)], recv1.at[pl.ds(0, n - 1)], sem_recv1).wait()

    send2[...] = jnp.sum(recv1[...].astype(F32), axis=0)

    deliver = pltpu.make_async_remote_copy(
        send2, recv2.at[z], sem_send2, sem_recv2, device_id={"narrow": w}, device_id_type=MESH
    )

    @pl.when(jnp.logical_not(owner))
    def _():
        deliver.start()
        deliver.wait_send()
        pltpu.make_async_copy(final, final, sem_recv3).wait()

    @pl.when(owner)
    def _():
        recv2[z] = send2[...]
        pltpu.make_async_copy(recv2.at[pl.ds(0, n - 1)], recv2.at[pl.ds(0, n - 1)], sem_recv2).wait()
        whole = jnp.sum(recv2[...], axis=0)
        send3[...] = whole
        final[...] = whole

        def hand_out(k, carry):
            pltpu.make_async_remote_copy(
                send3, final, sem_send3, sem_recv3, device_id={"wide": lax.rem(w + k, n)}, device_id_type=MESH
            ).start()
            return carry

        lax.fori_loop(1, n, hand_out, 0)
        pltpu.make_async_copy(recv2.at[pl.ds(0, n - 1)], recv2.at[pl.ds(0, n - 1)], sem_send3).wait()

    rows = C2 // n
    for t in range(TAPS):
        for r in range(rows):
            at = 8 * r + t // 4
            grad_ref[t, r : r + 1, :] = final[at : at + 1, C1 * (t % 4) : C1 * (t % 4) + C1]


def body(volumes, first_kernel, second_kernel, cotangent):
    n = lax.axis_size("wide")
    cells = cotangent.shape[3]
    scale = 1.0 / math.sqrt(n * lax.axis_size("narrow") * cells)
    size = C2 // n * 8
    vmem = pl.BlockSpec(memory_space=pltpu.VMEM)
    dma = pltpu.SemaphoreType.DMA
    inputs = (
        volumes.reshape(CIN, 4, 4096),
        jnp.asarray(lane_order(), BF16),
        jnp.asarray(row_order(), BF16),
        jnp.asarray(first_places(), BF16),
        first_kernel.transpose(0, 2, 1),
        second_kernel.transpose(0, 2, 1),
        cotangent.reshape(C2, cells),
    )
    act, grad = pl.pallas_call(
        functools.partial(kernel, n, scale),
        out_shape=(
            jax.ShapeDtypeStruct((C2, cells), BF16),
            jax.ShapeDtypeStruct((TAPS, C2 // n, C1), F32),
        ),
        in_specs=[pl.BlockSpec(memory_space=pltpu.HBM)] * 7,
        out_specs=(vmem, vmem),
        scratch_shapes=[
            *[pltpu.VMEM(x.shape, BF16) for x in inputs],
            dma((len(inputs),)),
            pltpu.VMEM((16, 4096), F32),
            pltpu.VMEM((128, C1), F32),
            pltpu.VMEM((144, PLANE), BF16),
            pltpu.VMEM((576, PLANE), BF16),
            pltpu.VMEM((4 * ROWS2 + 32, PLANE), BF16),
            pltpu.VMEM((C2, WIDTH), BF16),
            pltpu.VMEM((C2 * 8, 128), F32),
            pltpu.VMEM((n, size, 128), BF16),
            pltpu.VMEM((n, size, 128), BF16),
            pltpu.VMEM((size, 128), F32),
            pltpu.VMEM((n, size, 128), F32),
            pltpu.VMEM((size, 128), F32),
            pltpu.VMEM((size, 128), F32),
            dma((2,)),
            dma((2,)),
            dma(()),
            dma(()),
            dma(()),
            dma(()),
            dma(()),
            dma(()),
            pltpu.SemaphoreType.REGULAR,
        ],
        compiler_params=pltpu.CompilerParams(collective_id=0, has_side_effects=True, vmem_limit_bytes=24 << 20),
    )(*[pltpu.with_memory_space_constraint(x, pltpu.HBM) for x in inputs])
    return act.reshape(1, 1, C2, cells), grad


def solution(mesh):
    return jax.shard_map(
        body,
        mesh=mesh,
        in_specs=(P("narrow", None, None, "wide", None), P(), P(), P("narrow", None, None, "wide")),
        out_specs=(P("narrow", None, None, "wide"), P(None, "narrow", None)),
        check_vma=False,
    )
```

```python
import functools
import math

import jax
import jax.numpy as jnp
import numpy as np
from jax import lax
from jax.experimental import pallas as pl
from jax.experimental.pallas import tpu as pltpu
from jax.sharding import PartitionSpec as P

CIN = 4
C1 = 32
C2 = 64
HALF = 32
PLANE = HALF * HALF
SLOPE = 0.3
TAPS = 27
WIDTH = 896
ROWS2 = 9 * C1
F32 = jnp.float32
BF16 = jnp.bfloat16
MESH = pl.DeviceIdType.MESH


def lane_order():
    order = np.zeros((512, 512), np.float32)
    for k in range(4):
        for py in range(2):
            for x in range(64):
                order[k * 128 + py * 64 + x, (py * 2 + x % 2) * 128 + k * 32 + x // 2] = 1.0
    return order


def row_order():
    order = np.zeros((64, 64), np.float32)
    for z in range(4):
        for q in range(4):
            for ch in range(CIN):
                order[z * 16 + q * 4 + ch, q * 16 + ch * 4 + z] = 1.0
    return order


def first_places():
    places = np.zeros((256, 128), np.float32)
    for t in range(TAPS):
        a, b, c = t // 9, t // 3 % 3, t % 3
        shift = (2 if b == 0 else 0) + (1 if c == 0 else 0)
        q = (0 if b == 1 else 2) + (0 if c == 1 else 1)
        for i in range(CIN):
            places[a * 64 + shift * 16 + q * 4 + i, CIN * t + i] = 1.0
    return places


def rolled(x, shift):
    return pltpu.roll(x, shift % PLANE, axis=1)


def turned(x, size, kind=BF16):
    rows = lax.broadcasted_iota(jnp.int32, (size, size), 0)
    columns = lax.broadcasted_iota(jnp.int32, (size, size), 1)
    same = jnp.where(rows == columns, 1.0, 0.0).astype(BF16)
    return lax.dot_general(same, x, (((1,), (1,)), ((), ())), preferred_element_type=F32).astype(kind)


def kernel(
    n, scale, vol_hbm, lanes_hbm, rows_hbm, places_hbm, k1_hbm, k2_hbm, cot_hbm,
    act_ref, grad_ref,
    vol_ref, lanes_ref, rows_ref, places_ref, k1_ref, k2_ref, cot_ref, loads,
    raw, stacked, planes, taps1, taps2, weights2, spread, send1, recv1, send2, recv2, send3, final,
    halo_send, halo_recv, sem_send1, sem_recv1, sem_send2, sem_recv2, sem_send3, sem_recv3,
    ready_a, ready_b, meet_x, meet_y, meet_far, meet_core,
):
    w = lax.axis_index("wide")
    z = lax.axis_index("narrow")
    core = lax.rem(w, 2)
    even, odd = core == 0, core == 1
    owner = z == w
    across = min(4, n // 2)
    along = n // 2 // across
    x = lax.rem(w // 2, across)
    y = w // (2 * across)
    partner = w + 1 - 2 * core
    row_mates = [(y * across + lax.rem(x + k, across)) * 2 + core for k in sorted({1, across - 1} - {0})]
    column_mates = [(lax.rem(y + k, along) * across + x) * 2 + core for k in sorted({1, along - 1} - {0}) if along > 1]
    first = w == 0
    last = w == n - 1
    barrier = pltpu.get_barrier_semaphore()

    def tell(semaphore, to):
        pl.semaphore_signal(semaphore, 1, device_id=to, device_id_type=MESH)

    @pl.when(jnp.logical_not(first))
    def _():
        tell(barrier, {"wide": w - 1})

    @pl.when(jnp.logical_not(last))
    def _():
        tell(barrier, {"wide": w + 1})

    for mate in row_mates + column_mates:
        tell(barrier, {"wide": mate})

    home_a = w - core
    home_b = w - core + 1

    def forwards(at, home):
        gap = lax.rem(at - home + 2 * n, n)
        reach = jnp.where(home > n // 2, n // 2, n - 1 - home)
        return gap < reach, jnp.where(gap == 0, reach < n - 1, gap > reach + 1)

    def sides(at):
        up_a, down_a = forwards(at, home_a)
        up_b, down_b = forwards(at, home_b)
        return odd & (up_a | up_b), odd & (down_a | down_b)

    above = lax.rem(z + 1, n)
    below = lax.rem(z + n - 1, n)

    @pl.when(sides(below)[0])
    def _():
        tell(barrier, {"narrow": below})

    @pl.when(sides(above)[1])
    def _():
        tell(barrier, {"narrow": above})

    expects_above, expects_below = sides(z)

    def meet(semaphore, mates):
        for mate in mates:
            tell(semaphore, {"wide": mate})

    def met(semaphore, mates):
        if mates:
            pl.semaphore_wait(semaphore, len(mates))

    def announce(semaphore, home):
        up, down = forwards(z, home)

        @pl.when(up)
        def _():
            tell(semaphore, {"narrow": above})

        @pl.when(down)
        def _():
            tell(semaphore, {"narrow": below})

    def pass_on(semaphore, home):
        @pl.when(z != home)
        def _():
            pl.semaphore_wait(semaphore, 1)
            announce(semaphore, home)

    def relay():
        @pl.when(odd)
        def _():
            pass_on(ready_a, home_a)

            @pl.when(z != home_a)
            def _():
                tell(ready_a, {"wide": partner})

            pass_on(ready_b, home_b)

        @pl.when(even & jnp.logical_not(owner))
        def _():
            pl.semaphore_wait(ready_a, 1)

    pairs = (
        (vol_hbm, vol_ref), (lanes_hbm, lanes_ref), (rows_hbm, rows_ref), (places_hbm, places_ref),
        (k1_hbm, k1_ref), (k2_hbm, k2_ref), (cot_hbm, cot_ref),
    )
    copies = [pltpu.make_async_copy(source, target, loads.at[i]) for i, (source, target) in enumerate(pairs)]
    for copy in copies:
        copy.start()

    greeted = len(row_mates) + len(column_mates)
    for expected in (w > 0, w < n - 1, expects_above, expects_below):
        greeted = greeted + jnp.where(expected, 1, 0)
    pl.semaphore_wait(barrier, greeted)
    meet(meet_x, row_mates)

    @pl.when(odd & (z == home_a))
    def _():
        announce(ready_a, home_a)

    @pl.when(odd & (z == home_b))
    def _():
        announce(ready_b, home_b)

    for copy in copies[:3]:
        copy.wait()
    for ch in range(CIN):
        raw[4 * ch : 4 * ch + 4, :] = vol_ref[ch].astype(F32)
    blocks = [raw[:, 512 * j : 512 * j + 512].astype(BF16) for j in range(8)]
    spreadout = jnp.dot(jnp.concatenate(blocks, axis=0), lanes_ref[...], preferred_element_type=F32).astype(BF16)
    joined = jnp.concatenate(
        [
            jnp.concatenate([spreadout[16 * j : 16 * j + 16, 128 * q : 128 * q + 128] for j in range(8)], axis=1)
            for q in range(4)
        ],
        axis=0,
    )
    planes[48:112, :] = jnp.dot(rows_ref[...], joined, preferred_element_type=F32).astype(BF16)

    @pl.when(first)
    def _():
        planes[0:48, :] = jnp.zeros((48, PLANE), BF16)

    @pl.when(last)
    def _():
        planes[112:144, :] = jnp.zeros((32, PLANE), BF16)

    upward = pltpu.make_async_remote_copy(
        planes.at[64:112], planes.at[0:48], halo_send.at[0], halo_recv.at[0],
        device_id={"wide": lax.rem(w + 1, n)}, device_id_type=MESH,
    )
    downward = pltpu.make_async_remote_copy(
        planes.at[48:80], planes.at[112:144], halo_send.at[1], halo_recv.at[1],
        device_id={"wide": lax.rem(w + n - 1, n)}, device_id_type=MESH,
    )

    @pl.when(jnp.logical_not(last))
    def _():
        upward.start()

    @pl.when(jnp.logical_not(first))
    def _():
        downward.start()

    met(meet_x, row_mates)
    meet(meet_y, column_mates)

    for copy in copies[3:]:
        copy.wait()
    for t in range(TAPS):
        stacked[CIN * t : CIN * t + CIN, :] = k1_ref[t].astype(F32)
    stacked[CIN * TAPS :, :] = jnp.zeros((128 - CIN * TAPS, C1), F32)
    placed = jnp.dot(places_ref[...], stacked[...].astype(BF16), preferred_element_type=F32).astype(BF16)
    weights1 = turned(placed, C1)[:, :192]
    weights2[:, : TAPS * C1] = turned(k2_ref[...].reshape(TAPS * C1, C2), C2)
    weights2[:, TAPS * C1 :] = jnp.zeros((C2, WIDTH - TAPS * C1), BF16)

    lane = lax.broadcasted_iota(jnp.int32, (16, PLANE), 1)
    left_ok = (lane % HALF) != 0
    lower_ok = lane >= HALF

    def spread_plane(zi):
        base = planes[16 * zi : 16 * zi + 16, :].astype(F32)
        at_x = jnp.where(left_ok, rolled(base, 1), 0.0)
        at_y = jnp.where(lower_ok, rolled(base, HALF), 0.0)
        both = jnp.where(lower_ok, rolled(at_x, HALF), 0.0)
        for s, part in enumerate((base, at_x, at_y, both)):
            taps1[64 * zi + 16 * s : 64 * zi + 16 * s + 16, :] = part.astype(BF16)

    for zi in range(3, 7):
        spread_plane(zi)
    taps2[4 * ROWS2 :, :] = jnp.zeros((32, PLANE), BF16)
    taps2[3 * ROWS2 : 3 * ROWS2 + 32, :] = jnp.zeros((32, PLANE), BF16)

    lane2 = lax.broadcasted_iota(jnp.int32, (C1, PLANE), 1)
    left2 = (lane2 % HALF) != 0
    right2 = (lane2 % HALF) != HALF - 1
    lower2 = lane2 >= HALF
    upper2 = lane2 < PLANE - HALF

    def first_layer(zo):
        pre = jnp.dot(weights1, taps1[128 * zo : 128 * zo + 192, :], preferred_element_type=F32)
        act = jnp.where(pre > 0, pre, SLOPE * pre)
        if zo == 3:
            act = jnp.where(last, 0.0, act)
        act = act.astype(BF16).astype(F32)
        shifted = (jnp.where(left2, rolled(act, 1), 0.0), act, jnp.where(right2, rolled(act, -1), 0.0))
        for c in range(3):
            parts = (
                jnp.where(lower2, rolled(shifted[c], HALF), 0.0),
                shifted[c],
                jnp.where(upper2, rolled(shifted[c], -HALF), 0.0),
            )
            for b in range(3):
                row = ROWS2 * zo + C1 * (3 * b + c)
                taps2[row : row + C1, :] = parts[b].astype(BF16)

    def second_layer(half):
        patches = taps2[ROWS2 * half : ROWS2 * half + WIDTH, :]
        pre = jnp.dot(weights2[...], patches, preferred_element_type=F32)
        cells = slice(PLANE * half, PLANE * half + PLANE)
        act_ref[:, cells] = jnp.where(pre > 0, pre, SLOPE * pre).astype(BF16)
        back = (cot_ref[:, cells].astype(F32) * jnp.where(pre > 0, 1.0, SLOPE)).astype(BF16)
        return lax.dot_general(patches, back, (((1,), (1,)), ((), ())), preferred_element_type=F32)

    first_layer(2)
    met(meet_y, column_mates)
    meet(meet_far, column_mates)

    @pl.when(jnp.logical_not(last))
    def _():
        upward.wait_send()
        downward.wait_recv()

    @pl.when(jnp.logical_not(first))
    def _():
        downward.wait_send()
        upward.wait_recv()

    for zi in (0, 1, 2, 7, 8):
        spread_plane(zi)
    met(meet_far, column_mates)
    tell(meet_core, {"wide": partner})
    first_layer(0)
    first_layer(1)
    total = second_layer(0)
    first_layer(3)
    total = total + second_layer(1)
    pl.semaphore_wait(meet_core, 1)

    total = turned((total * scale).astype(BF16), C2, F32)
    for k in range(7):
        spread[pl.ds(k, C2, stride=8), :] = total[:, 128 * k : 128 * k + 128]
    spread[pl.ds(7, C2, stride=8), :] = jnp.zeros((C2, 128), F32)
    size = C2 // n * 8
    send1[...] = spread[...].astype(BF16).reshape(n, size, 128)
    recv1[w] = send1[w]

    def scatter(k, carry):
        to = lax.rem(w + k, n)
        pltpu.make_async_remote_copy(
            send1.at[to], recv1.at[w], sem_send1, sem_recv1, device_id={"wide": to}, device_id_type=MESH
        ).start()
        return carry

    lax.fori_loop(1, n, scatter, 0)
    relay()
    pltpu.make_async_copy(send1.at[pl.ds(0, n - 1)], send1.at[pl.ds(0, n - 1)], sem_send1).wait()
    pltpu.make_async_copy(recv1.at[pl.ds(0, n - 1)], recv1.at[pl.ds(0, n - 1)], sem_recv1).wait()

    send2[...] = jnp.sum(recv1[...].astype(F32), axis=0).astype(BF16)

    deliver = pltpu.make_async_remote_copy(
        send2, recv2.at[z], sem_send2, sem_recv2, device_id={"narrow": w}, device_id_type=MESH
    )

    @pl.when(jnp.logical_not(owner))
    def _():
        deliver.start()
        deliver.wait_send()
        pltpu.make_async_copy(final, final, sem_recv3).wait()

    @pl.when(owner)
    def _():
        recv2[z] = send2[...]
        pltpu.make_async_copy(recv2.at[pl.ds(0, n - 1)], recv2.at[pl.ds(0, n - 1)], sem_recv2).wait()
        whole = jnp.sum(recv2[...].astype(F32), axis=0)
        send3[...] = whole
        final[...] = whole

        def hand_out(k, carry):
            pltpu.make_async_remote_copy(
                send3, final, sem_send3, sem_recv3, device_id={"wide": lax.rem(w + k, n)}, device_id_type=MESH
            ).start()
            return carry

        lax.fori_loop(1, n, hand_out, 0)
        def handed_out(k, carry):
            pltpu.make_async_copy(send3, send3, sem_send3).wait()
            return carry

        lax.fori_loop(1, n, handed_out, 0)

    rows = C2 // n
    for t in range(TAPS):
        for r in range(rows):
            at = 8 * r + t // 4
            grad_ref[t, r : r + 1, :] = final[at : at + 1, C1 * (t % 4) : C1 * (t % 4) + C1]


def body(volumes, first_kernel, second_kernel, cotangent):
    n = lax.axis_size("wide")
    cells = cotangent.shape[3]
    scale = 1.0 / math.sqrt(n * lax.axis_size("narrow") * cells)
    size = C2 // n * 8
    vmem = pl.BlockSpec(memory_space=pltpu.VMEM)
    dma = pltpu.SemaphoreType.DMA
    inputs = (
        volumes.reshape(CIN, 4, 4096),
        jnp.asarray(lane_order(), BF16),
        jnp.asarray(row_order(), BF16),
        jnp.asarray(first_places(), BF16),
        first_kernel.transpose(0, 2, 1),
        second_kernel.transpose(0, 2, 1),
        cotangent.reshape(C2, cells),
    )
    act, grad = pl.pallas_call(
        functools.partial(kernel, n, scale),
        out_shape=(
            jax.ShapeDtypeStruct((C2, cells), BF16),
            jax.ShapeDtypeStruct((TAPS, C2 // n, C1), F32),
        ),
        in_specs=[pl.BlockSpec(memory_space=pltpu.HBM)] * 7,
        out_specs=(vmem, vmem),
        scratch_shapes=[
            *[pltpu.VMEM(x.shape, BF16) for x in inputs],
            dma((len(inputs),)),
            pltpu.VMEM((16, 4096), F32),
            pltpu.VMEM((128, C1), F32),
            pltpu.VMEM((144, PLANE), BF16),
            pltpu.VMEM((576, PLANE), BF16),
            pltpu.VMEM((4 * ROWS2 + 32, PLANE), BF16),
            pltpu.VMEM((C2, WIDTH), BF16),
            pltpu.VMEM((C2 * 8, 128), F32),
            pltpu.VMEM((n, size, 128), BF16),
            pltpu.VMEM((n, size, 128), BF16),
            pltpu.VMEM((size, 128), BF16),
            pltpu.VMEM((n, size, 128), BF16),
            pltpu.VMEM((size, 128), F32),
            pltpu.VMEM((size, 128), F32),
            dma((2,)),
            dma((2,)),
            dma(()),
            dma(()),
            dma(()),
            dma(()),
            dma(()),
            dma(()),
            *[pltpu.SemaphoreType.REGULAR] * 6,
        ],
        compiler_params=pltpu.CompilerParams(collective_id=0, has_side_effects=True, vmem_limit_bytes=24 << 20),
    )(*[pltpu.with_memory_space_constraint(x, pltpu.HBM) for x in inputs])
    return act.reshape(1, 1, C2, cells), grad


def solution(mesh):
    return jax.shard_map(
        body,
        mesh=mesh,
        in_specs=(P("narrow", None, None, "wide", None), P(), P(), P("narrow", None, None, "wide")),
        out_specs=(P("narrow", None, None, "wide"), P(None, "narrow", None)),
        check_vma=False,
    )
```

```python
import functools
import math

import jax
import jax.numpy as jnp
import numpy as np
from jax import lax
from jax.experimental import pallas as pl
from jax.experimental.pallas import tpu as pltpu
from jax.sharding import PartitionSpec as P

CIN = 4
C1 = 32
C2 = 64
HALF = 32
PLANE = HALF * HALF
SLOPE = 0.3
TAPS = 27
ROWS2 = 9 * C1
F32 = jnp.float32
BF16 = jnp.bfloat16
MESH = pl.DeviceIdType.MESH


def row_order():
    order = np.zeros((64, 64), np.float32)
    for z in range(4):
        for q in range(4):
            for ch in range(CIN):
                order[z * 16 + q * 4 + ch, q * 16 + ch * 4 + z] = 1.0
    return order


def first_places():
    places = np.zeros((256, 128), np.float32)
    for t in range(TAPS):
        a, b, c = t // 9, t // 3 % 3, t % 3
        shift = (2 if b == 0 else 0) + (1 if c == 0 else 0)
        q = (0 if b == 1 else 2) + (0 if c == 1 else 1)
        for i in range(CIN):
            places[a * 64 + shift * 16 + q * 4 + i, CIN * t + i] = 1.0
    return places


def rolled(x, shift):
    return pltpu.roll(x, shift % PLANE, axis=1)


def turned(x, size, kind=BF16):
    rows = lax.broadcasted_iota(jnp.int32, (size, size), 0)
    columns = lax.broadcasted_iota(jnp.int32, (size, size), 1)
    same = jnp.where(rows == columns, 1.0, 0.0).astype(BF16)
    return lax.dot_general(same, x, (((1,), (1,)), ((), ())), preferred_element_type=F32).astype(kind)


def kernel(
    n, scale, vol_hbm, rows_hbm, places_hbm, k1_hbm, k2_hbm, cot_hbm,
    act_ref, grad_ref,
    vol_ref, rows_ref, places_ref, k1_ref, k2_ref, cot_ref, loads,
    raw, stacked, planes, taps1, taps2, weights2, parts2, backs, spread, send1, recv1, send2, recv2, send3, final,
    halo_send, halo_recv, sem_send1, sem_recv1, sem_send2, sem_recv2, sem_send3, sem_recv3,
    ready_a, ready_b, wrap_ok, meet_x, meet_y, meet_far, meet_core,
):
    w = lax.axis_index("wide")
    z = lax.axis_index("narrow")
    core = lax.rem(w, 2)
    even, odd = core == 0, core == 1
    owner = z == w
    across = min(4, n // 2)
    along = n // 2 // across
    x = lax.rem(w // 2, across)
    y = w // (2 * across)
    partner = w + 1 - 2 * core
    row_mates = [(y * across + lax.rem(x + k, across)) * 2 + core for k in sorted({1, across - 1} - {0})]
    column_mates = [(lax.rem(y + k, along) * across + x) * 2 + core for k in sorted({1, along - 1} - {0}) if along > 1]
    first = w == 0
    last = w == n - 1
    barrier = pltpu.get_barrier_semaphore()

    def tell(semaphore, to):
        pl.semaphore_signal(semaphore, 1, device_id=to, device_id_type=MESH)

    @pl.when(jnp.logical_not(first))
    def _():
        tell(barrier, {"wide": w - 1})

    @pl.when(jnp.logical_not(last))
    def _():
        tell(barrier, {"wide": w + 1})

    for mate in row_mates + column_mates:
        tell(barrier, {"wide": mate})

    home_a = w - core
    home_b = w - core + 1

    turn = min(n - 1, 26 * n // 32)

    def forwards(at, home):
        gap = lax.rem(at - home + 2 * n, n)
        reach = jnp.where(home > n // 2, n // 2, turn - home)
        return gap < reach, jnp.where(gap == 0, reach < n - 1, gap > reach + 1)

    def sides(at):
        up_a, down_a = forwards(at, home_a)
        up_b, down_b = forwards(at, home_b)
        return odd & (up_a | up_b), odd & (down_a | down_b) & (at != 0)

    above = lax.rem(z + 1, n)
    below = lax.rem(z + n - 1, n)

    @pl.when(sides(below)[0])
    def _():
        tell(barrier, {"narrow": below})

    @pl.when(sides(above)[1])
    def _():
        tell(barrier, {"narrow": above})

    expects_above, expects_below = sides(z)

    wrap_a, wrap_b = forwards(0, home_a)[1], forwards(0, home_b)[1]
    wraps = odd & (wrap_a | wrap_b)

    @pl.when(wraps & (z == 0))
    def _():
        tell(barrier, {"narrow": n - 1})

    expects_first = wraps & (z == n - 1)

    def meet(semaphore, mates):
        for mate in mates:
            tell(semaphore, {"wide": mate})

    def met(semaphore, mates):
        if mates:
            pl.semaphore_wait(semaphore, len(mates))

    def announce(semaphore, home):
        up, down = forwards(z, home)

        @pl.when(up)
        def _():
            tell(semaphore, {"narrow": above})

        @pl.when(down & (z > 0))
        def _():
            tell(semaphore, {"narrow": below})

    def pass_on(semaphore, home):
        @pl.when(z != home)
        def _():
            pl.semaphore_wait(semaphore, 1)
            announce(semaphore, home)

    def relay():
        @pl.when(odd)
        def _():
            pass_on(ready_a, home_a)

            @pl.when(z != home_a)
            def _():
                tell(ready_a, {"wide": partner})

            @pl.when(wraps & (z == 0))
            def _():
                pl.semaphore_wait(wrap_ok, 1)

            @pl.when(wrap_a & (z == 0))
            def _():
                tell(ready_a, {"narrow": n - 1})

            pass_on(ready_b, home_b)

            @pl.when(wrap_b & (z == 0))
            def _():
                tell(ready_b, {"narrow": n - 1})

        @pl.when(even & jnp.logical_not(owner))
        def _():
            pl.semaphore_wait(ready_a, 1)

    pairs = (
        (vol_hbm, vol_ref), (rows_hbm, rows_ref), (places_hbm, places_ref),
        (k1_hbm, k1_ref), (k2_hbm, k2_ref), (cot_hbm, cot_ref),
    )
    copies = [pltpu.make_async_copy(source, target, loads.at[i]) for i, (source, target) in enumerate(pairs)]
    for copy in copies:
        copy.start()

    greeted = len(row_mates) + len(column_mates)
    for expected in (w > 0, w < n - 1, expects_above, expects_below, expects_first):
        greeted = greeted + jnp.where(expected, 1, 0)
    pl.semaphore_wait(barrier, greeted)
    meet(meet_x, row_mates)

    @pl.when(expects_first)
    def _():
        tell(wrap_ok, {"narrow": 0})

    @pl.when(odd & (z == home_a))
    def _():
        announce(ready_a, home_a)

    @pl.when(odd & (z == home_b))
    def _():
        announce(ready_b, home_b)

    source = lax.broadcasted_iota(jnp.int32, (512, 512), 0)
    target = lax.broadcasted_iota(jnp.int32, (512, 512), 1)
    goal = ((source // 64) % 2) * 256 + (source % 2) * 128 + (source // 128) * 32 + (source % 64) // 2
    lanes = jnp.where(goal == target, 1.0, 0.0).astype(BF16)
    for copy in copies[:2]:
        copy.wait()
    for ch in range(CIN):
        raw[4 * ch : 4 * ch + 4, :] = vol_ref[ch].astype(F32)
    blocks = [raw[:, 512 * j : 512 * j + 512].astype(BF16) for j in range(8)]
    spreadout = jnp.dot(jnp.concatenate(blocks, axis=0), lanes, preferred_element_type=F32).astype(BF16)
    joined = jnp.concatenate(
        [
            jnp.concatenate([spreadout[16 * j : 16 * j + 16, 128 * q : 128 * q + 128] for j in range(8)], axis=1)
            for q in range(4)
        ],
        axis=0,
    )
    planes[48:112, :] = jnp.dot(rows_ref[...], joined, preferred_element_type=F32).astype(BF16)

    @pl.when(first)
    def _():
        planes[0:48, :] = jnp.zeros((48, PLANE), BF16)

    @pl.when(last)
    def _():
        planes[112:144, :] = jnp.zeros((32, PLANE), BF16)

    upward = pltpu.make_async_remote_copy(
        planes.at[64:112], planes.at[0:48], halo_send.at[0], halo_recv.at[0],
        device_id={"wide": lax.rem(w + 1, n)}, device_id_type=MESH,
    )
    downward = pltpu.make_async_remote_copy(
        planes.at[48:80], planes.at[112:144], halo_send.at[1], halo_recv.at[1],
        device_id={"wide": lax.rem(w + n - 1, n)}, device_id_type=MESH,
    )

    @pl.when(jnp.logical_not(last))
    def _():
        upward.start()

    @pl.when(jnp.logical_not(first))
    def _():
        downward.start()

    met(meet_x, row_mates)
    meet(meet_y, column_mates)

    for copy in copies[2:]:
        copy.wait()
    for t in range(TAPS):
        stacked[CIN * t : CIN * t + CIN, :] = k1_ref[t].astype(F32)
    stacked[CIN * TAPS :, :] = jnp.zeros((128 - CIN * TAPS, C1), F32)
    placed = jnp.dot(places_ref[...], stacked[...].astype(BF16), preferred_element_type=F32).astype(BF16)
    weights1 = turned(placed, C1)[:, :192]
    for a in range(3):
        weights2[C2 * a : C2 * a + C2, :] = turned(k2_ref[9 * a : 9 * a + 9].reshape(ROWS2, C2), C2)

    lane = lax.broadcasted_iota(jnp.int32, (16, PLANE), 1)
    left_ok = (lane % HALF) != 0
    lower_ok = lane >= HALF

    def spread_plane(zi):
        base = planes[16 * zi : 16 * zi + 16, :].astype(F32)
        at_x = jnp.where(left_ok, rolled(base, 1), 0.0)
        at_y = jnp.where(lower_ok, rolled(base, HALF), 0.0)
        both = jnp.where(lower_ok, rolled(at_x, HALF), 0.0)
        for s, part in enumerate((base, at_x, at_y, both)):
            taps1[64 * zi + 16 * s : 64 * zi + 16 * s + 16, :] = part.astype(BF16)

    for zi in range(3, 7):
        spread_plane(zi)

    lane2 = lax.broadcasted_iota(jnp.int32, (C1, PLANE), 1)
    left2 = (lane2 % HALF) != 0
    right2 = (lane2 % HALF) != HALF - 1
    lower2 = lane2 >= HALF
    upper2 = lane2 < PLANE - HALF

    def first_layer(zo):
        pre = jnp.dot(weights1, taps1[128 * zo : 128 * zo + 192, :], preferred_element_type=F32)
        act = jnp.where(pre > 0, pre, SLOPE * pre)
        if zo == 3:
            act = jnp.where(last, 0.0, act)
        act = act.astype(BF16).astype(F32)
        shifted = (jnp.where(left2, rolled(act, 1), 0.0), act, jnp.where(right2, rolled(act, -1), 0.0))
        for c in range(3):
            parts = (
                jnp.where(lower2, rolled(shifted[c], HALF), 0.0),
                shifted[c],
                jnp.where(upper2, rolled(shifted[c], -HALF), 0.0),
            )
            for b in range(3):
                row = ROWS2 * zo + C1 * (3 * b + c)
                taps2[row : row + C1, :] = parts[b].astype(BF16)

    reached = [[a for a in range(3) if 0 <= zo - a <= 1] for zo in range(4)]

    def second_part(zo):
        low, count = reached[zo][0], len(reached[zo])
        parts2[zo, : C2 * count, :] = jnp.dot(
            weights2[C2 * low : C2 * (low + count), :], taps2[ROWS2 * zo : ROWS2 * zo + ROWS2, :],
            preferred_element_type=F32,
        )

    def second_sum(half):
        pre = None
        for a in range(3):
            at = C2 * reached[half + a].index(a)
            part = parts2[half + a, at : at + C2, :]
            pre = part if pre is None else pre + part
        cells = slice(PLANE * half, PLANE * half + PLANE)
        act_ref[:, cells] = jnp.where(pre > 0, pre, SLOPE * pre).astype(BF16)
        backs[half] = (cot_ref[:, cells].astype(F32) * jnp.where(pre > 0, 1.0, SLOPE)).astype(BF16)

    def gradient_part(zo):
        columns = jnp.concatenate(
            [backs[zo - a] if a in reached[zo] else jnp.zeros((C2, PLANE), BF16) for a in range(3)], axis=0
        )
        patches = taps2[ROWS2 * zo : ROWS2 * zo + ROWS2, :]
        return lax.dot_general(patches, columns, (((1,), (1,)), ((), ())), preferred_element_type=F32)

    first_layer(2)
    second_part(2)
    met(meet_y, column_mates)
    meet(meet_far, column_mates)

    @pl.when(jnp.logical_not(last))
    def _():
        upward.wait_send()
        downward.wait_recv()

    @pl.when(jnp.logical_not(first))
    def _():
        downward.wait_send()
        upward.wait_recv()

    for zi in (0, 1, 2, 7, 8):
        spread_plane(zi)
    met(meet_far, column_mates)
    tell(meet_core, {"wide": partner})
    for zo in (0, 1):
        first_layer(zo)
        second_part(zo)
    second_sum(0)
    first_layer(3)
    second_part(3)
    second_sum(1)
    total = gradient_part(0) + gradient_part(1) + gradient_part(2) + gradient_part(3)
    total = (total * scale).astype(BF16)
    total = jnp.concatenate([total[:, C2 * a : C2 * a + C2] for a in range(3)], axis=0)
    total = turned(total, C2, F32)
    pl.semaphore_wait(meet_core, 1)

    for k in range(6):
        spread[pl.ds(k, C2, stride=8), :] = total[:, 128 * k : 128 * k + 128]
    rest = jnp.concatenate([total[:, 768:], jnp.zeros((C2, 896 - TAPS * C1), F32)], axis=1)
    spread[pl.ds(6, C2, stride=8), :] = rest
    spread[pl.ds(7, C2, stride=8), :] = jnp.zeros((C2, 128), F32)
    size = C2 // n * 8
    send1[...] = spread[...].astype(BF16).reshape(n, size, 128)
    recv1[w] = send1[w]

    far = [min(d, along - d) for d in range(along)], [min(d, across - d) for d in range(across)]
    offsets = [(dy, dx, dc) for dy in range(along) for dx in range(across) for dc in range(2)][1:]
    y_at = [lax.rem(y + d, along) * (2 * across) for d in range(along)]
    x_at = [lax.rem(x + d, across) * 2 for d in range(across)]
    core_at = [core, 1 - core]
    order = sorted(offsets, key=lambda d: -(2 * far[0][d[0]] + 2 * far[1][d[1]] + d[2]))
    mates = [y_at[dy] + x_at[dx] + core_at[dc] for dy, dx, dc in order]
    for to in mates:
        pltpu.make_async_remote_copy(
            send1.at[to], recv1.at[w], sem_send1, sem_recv1, device_id={"wide": to}, device_id_type=MESH
        ).start()
    relay()
    pltpu.make_async_copy(send1.at[pl.ds(0, n - 1)], send1.at[pl.ds(0, n - 1)], sem_send1).wait()
    pltpu.make_async_copy(recv1.at[pl.ds(0, n - 1)], recv1.at[pl.ds(0, n - 1)], sem_recv1).wait()

    send2[...] = jnp.sum(recv1[...].astype(F32), axis=0).astype(BF16)

    deliver = pltpu.make_async_remote_copy(
        send2, recv2.at[z], sem_send2, sem_recv2, device_id={"narrow": w}, device_id_type=MESH
    )

    @pl.when(jnp.logical_not(owner))
    def _():
        deliver.start()
        deliver.wait_send()
        pltpu.make_async_copy(final, final, sem_recv3).wait()

    @pl.when(owner)
    def _():
        recv2[z] = send2[...]
        pltpu.make_async_copy(recv2.at[pl.ds(0, n - 1)], recv2.at[pl.ds(0, n - 1)], sem_recv2).wait()
        whole = jnp.sum(recv2[...].astype(F32), axis=0).astype(BF16)
        send3[...] = whole
        final[...] = whole

        for to in mates:
            pltpu.make_async_remote_copy(
                send3, final, sem_send3, sem_recv3, device_id={"wide": to}, device_id_type=MESH
            ).start()

        pltpu.make_async_copy(recv2.at[pl.ds(0, n - 1)], recv2.at[pl.ds(0, n - 1)], sem_send3).wait()

    rows = C2 // n
    result = final[...].astype(F32)
    for t in range(TAPS):
        for r in range(rows):
            at = 8 * r + t // 4
            grad_ref[t, r : r + 1, :] = result[at : at + 1, C1 * (t % 4) : C1 * (t % 4) + C1]


def body(volumes, first_kernel, second_kernel, cotangent):
    n = lax.axis_size("wide")
    cells = cotangent.shape[3]
    scale = 1.0 / math.sqrt(n * lax.axis_size("narrow") * cells)
    size = C2 // n * 8
    vmem = pl.BlockSpec(memory_space=pltpu.VMEM)
    dma = pltpu.SemaphoreType.DMA
    inputs = (
        volumes.reshape(CIN, 4, 4096),
        jnp.asarray(row_order(), BF16),
        jnp.asarray(first_places(), BF16),
        first_kernel.transpose(0, 2, 1),
        second_kernel.transpose(0, 2, 1),
        cotangent.reshape(C2, cells),
    )
    act, grad = pl.pallas_call(
        functools.partial(kernel, n, scale),
        out_shape=(
            jax.ShapeDtypeStruct((C2, cells), BF16),
            jax.ShapeDtypeStruct((TAPS, C2 // n, C1), F32),
        ),
        in_specs=[pl.BlockSpec(memory_space=pltpu.HBM)] * len(inputs),
        out_specs=(vmem, vmem),
        scratch_shapes=[
            *[pltpu.VMEM(x.shape, BF16) for x in inputs],
            dma((len(inputs),)),
            pltpu.VMEM((16, 4096), F32),
            pltpu.VMEM((128, C1), F32),
            pltpu.VMEM((144, PLANE), BF16),
            pltpu.VMEM((576, PLANE), BF16),
            pltpu.VMEM((4 * ROWS2, PLANE), BF16),
            pltpu.VMEM((3 * C2, ROWS2), BF16),
            pltpu.VMEM((4, 2 * C2, PLANE), F32),
            pltpu.VMEM((2, C2, PLANE), BF16),
            pltpu.VMEM((C2 * 8, 128), F32),
            pltpu.VMEM((n, size, 128), BF16),
            pltpu.VMEM((n, size, 128), BF16),
            pltpu.VMEM((size, 128), BF16),
            pltpu.VMEM((n, size, 128), BF16),
            pltpu.VMEM((size, 128), BF16),
            pltpu.VMEM((size, 128), BF16),
            dma((2,)),
            dma((2,)),
            dma(()),
            dma(()),
            dma(()),
            dma(()),
            dma(()),
            dma(()),
            *[pltpu.SemaphoreType.REGULAR] * 7,
        ],
        compiler_params=pltpu.CompilerParams(collective_id=0, has_side_effects=True, vmem_limit_bytes=24 << 20),
    )(*[pltpu.with_memory_space_constraint(x, pltpu.HBM) for x in inputs])
    return act.reshape(1, 1, C2, cells), grad


def solution(mesh):
    return jax.shard_map(
        body,
        mesh=mesh,
        in_specs=(P("narrow", None, None, "wide", None), P(), P(), P("narrow", None, None, "wide")),
        out_specs=(P("narrow", None, None, "wide"), P(None, "narrow", None)),
        check_vma=False,
    )
```

```python
import functools
import math

import jax
import jax.numpy as jnp
import numpy as np
from jax import lax
from jax.experimental import pallas as pl
from jax.experimental.pallas import tpu as pltpu
from jax.sharding import PartitionSpec as P

CIN = 4
C1 = 32
C2 = 64
HALF = 32
PLANE = HALF * HALF
SLOPE = 0.3
TAPS = 27
ROWS2 = 9 * C1
F32 = jnp.float32
BF16 = jnp.bfloat16
MESH = pl.DeviceIdType.MESH


def row_order():
    order = np.zeros((64, 64), np.float32)
    for z in range(4):
        for q in range(4):
            for ch in range(CIN):
                order[z * 16 + q * 4 + ch, q * 16 + ch * 4 + z] = 1.0
    return order


def first_places():
    places = np.zeros((256, 128), np.float32)
    for t in range(TAPS):
        a, b, c = t // 9, t // 3 % 3, t % 3
        shift = (2 if b == 0 else 0) + (1 if c == 0 else 0)
        q = (0 if b == 1 else 2) + (0 if c == 1 else 1)
        for i in range(CIN):
            places[a * 64 + shift * 16 + q * 4 + i, CIN * t + i] = 1.0
    return places


def rolled(x, shift):
    return pltpu.roll(x, shift % PLANE, axis=1)


def turned(x, size, kind=BF16):
    rows = lax.broadcasted_iota(jnp.int32, (size, size), 0)
    columns = lax.broadcasted_iota(jnp.int32, (size, size), 1)
    same = jnp.where(rows == columns, 1.0, 0.0).astype(BF16)
    return lax.dot_general(same, x, (((1,), (1,)), ((), ())), preferred_element_type=F32).astype(kind)


def kernel(
    n, scale, vol_hbm, rows_hbm, places_hbm, k1_hbm, k2_hbm, cot_hbm,
    act_ref, grad_ref,
    vol_ref, rows_ref, places_ref, k1_ref, k2_ref, cot_ref, loads,
    raw, stacked, planes, taps1, taps2, weights2, parts2, backs, spread, send1, recv1, send2, recv2, send3, final,
    halo_send, halo_recv, sem_send1, sem_recv1, sem_send2, sem_recv2, sem_send3, sem_recv3,
    ready_a, ready_b, wrap_ok, near1, near2, near3,
):
    w = lax.axis_index("wide")
    z = lax.axis_index("narrow")
    core = lax.rem(w, 2)
    even, odd = core == 0, core == 1
    owner = z == w
    across = min(4, n // 2)
    along = n // 2 // across
    x = lax.rem(w // 2, across)
    y = w // (2 * across)
    partner = w + 1 - 2 * core
    row_mates = [(y * across + lax.rem(x + k, across)) * 2 + core for k in sorted({1, across - 1} - {0})]
    column_mates = [(lax.rem(y + k, along) * across + x) * 2 + core for k in sorted({1, along - 1} - {0}) if along > 1]
    first = w == 0
    last = w == n - 1
    barrier = pltpu.get_barrier_semaphore()

    def tell(semaphore, to):
        pl.semaphore_signal(semaphore, 1, device_id=to, device_id_type=MESH)

    @pl.when(jnp.logical_not(first))
    def _():
        tell(barrier, {"wide": w - 1})

    @pl.when(jnp.logical_not(last))
    def _():
        tell(barrier, {"wide": w + 1})

    mates_near = row_mates + column_mates
    for mate in mates_near:
        tell(barrier, {"wide": mate})
        tell(barrier, {"wide": mate + 1 - 2 * core})

    home_a = w - core
    home_b = w - core + 1

    turn = min(n - 1, 3 * n // 4 + 1)

    def forwards(at, home):
        gap = lax.rem(at - home + 2 * n, n)
        reach = jnp.where(home > n // 2, n // 2, jnp.where(home == n // 2, n - 1, turn) - home)
        return gap < reach, jnp.where(gap == 0, reach < n - 1, gap > reach + 1)

    def sides(at):
        up_a, down_a = forwards(at, home_a)
        up_b, down_b = forwards(at, home_b)
        return odd & (up_a | up_b), odd & (down_a | down_b) & (at != 0)

    above = lax.rem(z + 1, n)
    below = lax.rem(z + n - 1, n)

    @pl.when(sides(below)[0])
    def _():
        tell(barrier, {"narrow": below})

    @pl.when(sides(above)[1])
    def _():
        tell(barrier, {"narrow": above})

    expects_above, expects_below = sides(z)

    wrap_a, wrap_b = forwards(0, home_a)[1], forwards(0, home_b)[1]
    wraps = odd & (wrap_a | wrap_b)

    @pl.when(wraps & (z == 0))
    def _():
        tell(barrier, {"narrow": n - 1})

    expects_first = wraps & (z == n - 1)

    def meet(semaphore, mates):
        for mate in mates:
            tell(semaphore, {"wide": mate})

    def met(semaphore, mates):
        if mates:
            pl.semaphore_wait(semaphore, len(mates))

    def announce(semaphore, home):
        up, down = forwards(z, home)

        @pl.when(up)
        def _():
            tell(semaphore, {"narrow": above})

        @pl.when(down & (z > 0))
        def _():
            tell(semaphore, {"narrow": below})

    def pass_on(semaphore, home):
        @pl.when(z != home)
        def _():
            pl.semaphore_wait(semaphore, 1)
            announce(semaphore, home)

    def relay():
        @pl.when(odd)
        def _():
            pass_on(ready_a, home_a)

            @pl.when(z != home_a)
            def _():
                tell(ready_a, {"wide": partner})

            @pl.when(wraps & (z == 0))
            def _():
                pl.semaphore_wait(wrap_ok, 1)

            @pl.when(wrap_a & (z == 0))
            def _():
                tell(ready_a, {"narrow": n - 1})

            pass_on(ready_b, home_b)

            @pl.when(wrap_b & (z == 0))
            def _():
                tell(ready_b, {"narrow": n - 1})

        @pl.when(even & jnp.logical_not(owner))
        def _():
            pl.semaphore_wait(ready_a, 1)

    pairs = (
        (vol_hbm, vol_ref), (rows_hbm, rows_ref), (places_hbm, places_ref),
        (k1_hbm, k1_ref), (k2_hbm, k2_ref), (cot_hbm, cot_ref),
    )
    copies = [pltpu.make_async_copy(source, target, loads.at[i]) for i, (source, target) in enumerate(pairs)]
    for copy in copies:
        copy.start()

    greeted = 2 * len(mates_near)
    for expected in (w > 0, w < n - 1, expects_above, expects_below, expects_first):
        greeted = greeted + jnp.where(expected, 1, 0)
    pl.semaphore_wait(barrier, greeted)
    meet(near1, mates_near)

    @pl.when(expects_first)
    def _():
        tell(wrap_ok, {"narrow": 0})

    @pl.when(odd & (z == home_a))
    def _():
        announce(ready_a, home_a)

    @pl.when(odd & (z == home_b))
    def _():
        announce(ready_b, home_b)

    source = lax.broadcasted_iota(jnp.int32, (512, 512), 0)
    target = lax.broadcasted_iota(jnp.int32, (512, 512), 1)
    goal = ((source // 64) % 2) * 256 + (source % 2) * 128 + (source // 128) * 32 + (source % 64) // 2
    lanes = jnp.where(goal == target, 1.0, 0.0).astype(BF16)
    for copy in copies[:2]:
        copy.wait()
    for ch in range(CIN):
        raw[4 * ch : 4 * ch + 4, :] = vol_ref[ch].astype(F32)
    blocks = [raw[:, 512 * j : 512 * j + 512].astype(BF16) for j in range(8)]
    spreadout = jnp.dot(jnp.concatenate(blocks, axis=0), lanes, preferred_element_type=F32).astype(BF16)
    joined = jnp.concatenate(
        [
            jnp.concatenate([spreadout[16 * j : 16 * j + 16, 128 * q : 128 * q + 128] for j in range(8)], axis=1)
            for q in range(4)
        ],
        axis=0,
    )
    planes[48:112, :] = jnp.dot(rows_ref[...], joined, preferred_element_type=F32).astype(BF16)

    @pl.when(first)
    def _():
        planes[0:48, :] = jnp.zeros((48, PLANE), BF16)

    @pl.when(last)
    def _():
        planes[112:144, :] = jnp.zeros((32, PLANE), BF16)

    upward = pltpu.make_async_remote_copy(
        planes.at[64:112], planes.at[0:48], halo_send.at[0], halo_recv.at[0],
        device_id={"wide": lax.rem(w + 1, n)}, device_id_type=MESH,
    )
    downward = pltpu.make_async_remote_copy(
        planes.at[48:80], planes.at[112:144], halo_send.at[1], halo_recv.at[1],
        device_id={"wide": lax.rem(w + n - 1, n)}, device_id_type=MESH,
    )

    @pl.when(jnp.logical_not(last))
    def _():
        upward.start()

    @pl.when(jnp.logical_not(first))
    def _():
        downward.start()

    met(near1, mates_near)
    meet(near2, mates_near)

    for copy in copies[2:]:
        copy.wait()
    for t in range(TAPS):
        stacked[CIN * t : CIN * t + CIN, :] = k1_ref[t].astype(F32)
    stacked[CIN * TAPS :, :] = jnp.zeros((128 - CIN * TAPS, C1), F32)
    placed = jnp.dot(places_ref[...], stacked[...].astype(BF16), preferred_element_type=F32).astype(BF16)
    weights1 = turned(placed, C1)[:, :192]
    for a in range(3):
        weights2[C2 * a : C2 * a + C2, :] = turned(k2_ref[9 * a : 9 * a + 9].reshape(ROWS2, C2), C2)

    lane = lax.broadcasted_iota(jnp.int32, (16, PLANE), 1)
    left_ok = (lane % HALF) != 0
    lower_ok = lane >= HALF

    def spread_plane(zi):
        base = planes[16 * zi : 16 * zi + 16, :].astype(F32)
        at_x = jnp.where(left_ok, rolled(base, 1), 0.0)
        at_y = jnp.where(lower_ok, rolled(base, HALF), 0.0)
        both = jnp.where(lower_ok, rolled(at_x, HALF), 0.0)
        for s, part in enumerate((base, at_x, at_y, both)):
            taps1[64 * zi + 16 * s : 64 * zi + 16 * s + 16, :] = part.astype(BF16)

    for zi in range(3, 7):
        spread_plane(zi)

    lane2 = lax.broadcasted_iota(jnp.int32, (C1, PLANE), 1)
    left2 = (lane2 % HALF) != 0
    right2 = (lane2 % HALF) != HALF - 1
    lower2 = lane2 >= HALF
    upper2 = lane2 < PLANE - HALF

    def first_layer(zo):
        pre = jnp.dot(weights1, taps1[128 * zo : 128 * zo + 192, :], preferred_element_type=F32)
        act = jnp.where(pre > 0, pre, SLOPE * pre)
        if zo == 3:
            act = jnp.where(last, 0.0, act)
        act = act.astype(BF16).astype(F32)
        shifted = (jnp.where(left2, rolled(act, 1), 0.0), act, jnp.where(right2, rolled(act, -1), 0.0))
        for c in range(3):
            parts = (
                jnp.where(lower2, rolled(shifted[c], HALF), 0.0),
                shifted[c],
                jnp.where(upper2, rolled(shifted[c], -HALF), 0.0),
            )
            for b in range(3):
                row = ROWS2 * zo + C1 * (3 * b + c)
                taps2[row : row + C1, :] = parts[b].astype(BF16)

    reached = [[a for a in range(3) if 0 <= zo - a <= 1] for zo in range(4)]

    def second_part(zo):
        low, count = reached[zo][0], len(reached[zo])
        parts2[zo, : C2 * count, :] = jnp.dot(
            weights2[C2 * low : C2 * (low + count), :], taps2[ROWS2 * zo : ROWS2 * zo + ROWS2, :],
            preferred_element_type=F32,
        )

    def second_sum(half):
        pre = None
        for a in range(3):
            at = C2 * reached[half + a].index(a)
            part = parts2[half + a, at : at + C2, :]
            pre = part if pre is None else pre + part
        cells = slice(PLANE * half, PLANE * half + PLANE)
        act_ref[:, cells] = jnp.where(pre > 0, pre, SLOPE * pre).astype(BF16)
        backs[half] = (cot_ref[:, cells].astype(F32) * jnp.where(pre > 0, 1.0, SLOPE)).astype(BF16)

    def gradient_part(zo):
        columns = jnp.concatenate(
            [backs[zo - a] if a in reached[zo] else jnp.zeros((C2, PLANE), BF16) for a in range(3)], axis=0
        )
        patches = taps2[ROWS2 * zo : ROWS2 * zo + ROWS2, :]
        return lax.dot_general(patches, columns, (((1,), (1,)), ((), ())), preferred_element_type=F32)

    first_layer(2)
    second_part(2)
    met(near2, mates_near)
    meet(near3, mates_near)

    @pl.when(jnp.logical_not(last))
    def _():
        upward.wait_send()
        downward.wait_recv()

    @pl.when(jnp.logical_not(first))
    def _():
        downward.wait_send()
        upward.wait_recv()

    for zi in (0, 1, 2, 7, 8):
        spread_plane(zi)
    for zo in (0, 1):
        first_layer(zo)
        second_part(zo)
    second_sum(0)
    first_layer(3)
    second_part(3)
    second_sum(1)
    total = gradient_part(0) + gradient_part(1) + gradient_part(2) + gradient_part(3)
    total = (total * scale).astype(BF16)
    total = jnp.concatenate([total[:, C2 * a : C2 * a + C2] for a in range(3)], axis=0)
    total = turned(total, C2, F32)
    met(near3, mates_near)

    for k in range(6):
        spread[pl.ds(k, C2, stride=8), :] = total[:, 128 * k : 128 * k + 128]
    rest = jnp.concatenate([total[:, 768:], jnp.zeros((C2, 896 - TAPS * C1), F32)], axis=1)
    spread[pl.ds(6, C2, stride=8), :] = rest
    spread[pl.ds(7, C2, stride=8), :] = jnp.zeros((C2, 128), F32)
    size = C2 // n * 8
    send1[...] = spread[...].astype(BF16).reshape(n, size, 128)
    recv1[w] = send1[w]

    far = [min(d, along - d) for d in range(along)], [min(d, across - d) for d in range(across)]
    offsets = [(dy, dx, dc) for dy in range(along) for dx in range(across) for dc in range(2)][1:]
    y_at = [lax.rem(y + d, along) * (2 * across) for d in range(along)]
    x_at = [lax.rem(x + d, across) * 2 for d in range(across)]
    core_at = [core, 1 - core]
    order = sorted(offsets, key=lambda d: -(2 * far[0][d[0]] + 2 * far[1][d[1]] + d[2]))
    mates = [y_at[dy] + x_at[dx] + core_at[dc] for dy, dx, dc in order]
    for to in mates:
        pltpu.make_async_remote_copy(
            send1.at[to], recv1.at[w], sem_send1, sem_recv1, device_id={"wide": to}, device_id_type=MESH
        ).start()
    relay()
    pltpu.make_async_copy(send1.at[pl.ds(0, n - 1)], send1.at[pl.ds(0, n - 1)], sem_send1).wait()
    pltpu.make_async_copy(recv1.at[pl.ds(0, n - 1)], recv1.at[pl.ds(0, n - 1)], sem_recv1).wait()

    send2[...] = jnp.sum(recv1[...].astype(F32), axis=0).astype(BF16)

    deliver = pltpu.make_async_remote_copy(
        send2, recv2.at[z], sem_send2, sem_recv2, device_id={"narrow": w}, device_id_type=MESH
    )

    @pl.when(jnp.logical_not(owner))
    def _():
        deliver.start()
        deliver.wait_send()
        pltpu.make_async_copy(final, final, sem_recv3).wait()

    @pl.when(owner)
    def _():
        recv2[z] = send2[...]
        pltpu.make_async_copy(recv2.at[pl.ds(0, n - 1)], recv2.at[pl.ds(0, n - 1)], sem_recv2).wait()
        whole = jnp.sum(recv2[...].astype(F32), axis=0).astype(BF16)
        send3[...] = whole
        final[...] = whole

        for to in mates:
            pltpu.make_async_remote_copy(
                send3, final, sem_send3, sem_recv3, device_id={"wide": to}, device_id_type=MESH
            ).start()

        pltpu.make_async_copy(recv2.at[pl.ds(0, n - 1)], recv2.at[pl.ds(0, n - 1)], sem_send3).wait()

    rows = C2 // n
    result = final[...].astype(F32)
    for t in range(TAPS):
        for r in range(rows):
            at = 8 * r + t // 4
            grad_ref[t, r : r + 1, :] = result[at : at + 1, C1 * (t % 4) : C1 * (t % 4) + C1]


def body(volumes, first_kernel, second_kernel, cotangent):
    n = lax.axis_size("wide")
    cells = cotangent.shape[3]
    scale = 1.0 / math.sqrt(n * lax.axis_size("narrow") * cells)
    size = C2 // n * 8
    vmem = pl.BlockSpec(memory_space=pltpu.VMEM)
    dma = pltpu.SemaphoreType.DMA
    inputs = (
        volumes.reshape(CIN, 4, 4096),
        jnp.asarray(row_order(), BF16),
        jnp.asarray(first_places(), BF16),
        first_kernel.transpose(0, 2, 1),
        second_kernel.transpose(0, 2, 1),
        cotangent.reshape(C2, cells),
    )
    act, grad = pl.pallas_call(
        functools.partial(kernel, n, scale),
        out_shape=(
            jax.ShapeDtypeStruct((C2, cells), BF16),
            jax.ShapeDtypeStruct((TAPS, C2 // n, C1), F32),
        ),
        in_specs=[pl.BlockSpec(memory_space=pltpu.HBM)] * len(inputs),
        out_specs=(vmem, vmem),
        scratch_shapes=[
            *[pltpu.VMEM(x.shape, BF16) for x in inputs],
            dma((len(inputs),)),
            pltpu.VMEM((16, 4096), F32),
            pltpu.VMEM((128, C1), F32),
            pltpu.VMEM((144, PLANE), BF16),
            pltpu.VMEM((576, PLANE), BF16),
            pltpu.VMEM((4 * ROWS2, PLANE), BF16),
            pltpu.VMEM((3 * C2, ROWS2), BF16),
            pltpu.VMEM((4, 2 * C2, PLANE), F32),
            pltpu.VMEM((2, C2, PLANE), BF16),
            pltpu.VMEM((C2 * 8, 128), F32),
            pltpu.VMEM((n, size, 128), BF16),
            pltpu.VMEM((n, size, 128), BF16),
            pltpu.VMEM((size, 128), BF16),
            pltpu.VMEM((n, size, 128), BF16),
            pltpu.VMEM((size, 128), BF16),
            pltpu.VMEM((size, 128), BF16),
            dma((2,)),
            dma((2,)),
            dma(()),
            dma(()),
            dma(()),
            dma(()),
            dma(()),
            dma(()),
            *[pltpu.SemaphoreType.REGULAR] * 6,
        ],
        compiler_params=pltpu.CompilerParams(collective_id=0, has_side_effects=True, vmem_limit_bytes=24 << 20),
    )(*[pltpu.with_memory_space_constraint(x, pltpu.HBM) for x in inputs])
    return act.reshape(1, 1, C2, cells), grad


def solution(mesh):
    return jax.shard_map(
        body,
        mesh=mesh,
        in_specs=(P("narrow", None, None, "wide", None), P(), P(), P("narrow", None, None, "wide")),
        out_specs=(P("narrow", None, None, "wide"), P(None, "narrow", None)),
        check_vma=False,
    )
```

```python
import functools
import math

import jax
import jax.numpy as jnp
import numpy as np
from jax import lax
from jax.experimental import pallas as pl
from jax.experimental.pallas import tpu as pltpu
from jax.sharding import PartitionSpec as P

CIN = 4
C1 = 32
C2 = 64
HALF = 32
PLANE = HALF * HALF
SLOPE = 0.3
TAPS = 27
ROWS2 = 9 * C1
F32 = jnp.float32
BF16 = jnp.bfloat16
MESH = pl.DeviceIdType.MESH


def row_order():
    order = np.zeros((64, 64), np.float32)
    for z in range(4):
        for q in range(4):
            for ch in range(CIN):
                order[z * 16 + q * 4 + ch, q * 16 + ch * 4 + z] = 1.0
    return order


def first_places():
    places = np.zeros((256, 128), np.float32)
    for t in range(TAPS):
        a, b, c = t // 9, t // 3 % 3, t % 3
        shift = (2 if b == 0 else 0) + (1 if c == 0 else 0)
        q = (0 if b == 1 else 2) + (0 if c == 1 else 1)
        for i in range(CIN):
            places[a * 64 + shift * 16 + q * 4 + i, CIN * t + i] = 1.0
    return places


def rolled(x, shift):
    return pltpu.roll(x, shift % PLANE, axis=1)


def turned(x, size, kind=BF16):
    rows = lax.broadcasted_iota(jnp.int32, (size, size), 0)
    columns = lax.broadcasted_iota(jnp.int32, (size, size), 1)
    same = jnp.where(rows == columns, 1.0, 0.0).astype(BF16)
    return lax.dot_general(same, x, (((1,), (1,)), ((), ())), preferred_element_type=F32).astype(kind)


def kernel(
    n, scale, vol_hbm, rows_hbm, places_hbm, k1_hbm, k2_hbm, cot_hbm,
    act_ref, grad_ref,
    vol_ref, rows_ref, places_ref, k1_ref, k2_ref, cot_ref, loads,
    raw, stacked, planes, taps1, taps2, weights2, parts2, backs, spread, send1, recv1, send2, recv2, send3, final,
    halo_send, halo_recv, sem_send1, sem_recv1, sem_send2, sem_recv2, sem_send3, sem_recv3,
    ready_a, ready_b, wrap_ok, near1, near2, near3,
):
    w = lax.axis_index("wide")
    z = lax.axis_index("narrow")
    core = lax.rem(w, 2)
    even, odd = core == 0, core == 1
    across = min(4, n // 2)
    along = n // 2 // across
    x = lax.rem(w // 2, across)
    y = w // (2 * across)
    partner = w + 1 - 2 * core
    row_mates = [(y * across + lax.rem(x + k, across)) * 2 + core for k in sorted({1, across - 1} - {0})]
    column_mates = [(lax.rem(y + k, along) * across + x) * 2 + core for k in sorted({1, along - 1} - {0}) if along > 1]
    first = w == 0
    last = w == n - 1
    barrier = pltpu.get_barrier_semaphore()

    def tell(semaphore, to):
        pl.semaphore_signal(semaphore, 1, device_id=to, device_id_type=MESH)

    @pl.when(jnp.logical_not(first))
    def _():
        tell(barrier, {"wide": w - 1})

    @pl.when(jnp.logical_not(last))
    def _():
        tell(barrier, {"wide": w + 1})

    mates_near = row_mates + column_mates
    for mate in mates_near:
        tell(barrier, {"wide": mate})
        tell(barrier, {"wide": mate + 1 - 2 * core})

    home_a = w - core
    home_b = w - core + 1
    own_a, own_b = odd & (z == home_a), odd & (z == home_b)
    owner = own_a | own_b

    turn = min(n - 1, 3 * n // 4 + 1)

    def forwards(at, home):
        gap = lax.rem(at - home + 2 * n, n)
        reach = jnp.where(home > n // 2, n // 2, jnp.where(home == n // 2, n - 1, turn) - home)
        return gap < reach, jnp.where(gap == 0, reach < n - 1, gap > reach + 1)

    def sides(at):
        up_a, down_a = forwards(at, home_a)
        up_b, down_b = forwards(at, home_b)
        return odd & (up_a | up_b), odd & (down_a | down_b) & (at != 0)

    above = lax.rem(z + 1, n)
    below = lax.rem(z + n - 1, n)

    @pl.when(sides(below)[0])
    def _():
        tell(barrier, {"narrow": below})

    @pl.when(sides(above)[1])
    def _():
        tell(barrier, {"narrow": above})

    expects_above, expects_below = sides(z)

    wrap_a, wrap_b = forwards(0, home_a)[1], forwards(0, home_b)[1]
    wraps = odd & (wrap_a | wrap_b)

    @pl.when(wraps & (z == 0))
    def _():
        tell(barrier, {"narrow": n - 1})

    expects_first = wraps & (z == n - 1)

    def meet(semaphore, mates):
        for mate in mates:
            tell(semaphore, {"wide": mate})

    def met(semaphore, mates):
        if mates:
            pl.semaphore_wait(semaphore, len(mates))

    def announce(semaphore, home):
        up, down = forwards(z, home)

        @pl.when(up)
        def _():
            tell(semaphore, {"narrow": above})

        @pl.when(down & (z > 0))
        def _():
            tell(semaphore, {"narrow": below})

    def pass_on(semaphore, home):
        @pl.when(z != home)
        def _():
            pl.semaphore_wait(semaphore, 1)
            announce(semaphore, home)

    def relay():
        @pl.when(odd)
        def _():
            pass_on(ready_a, home_a)

            @pl.when(z != home_a)
            def _():
                tell(ready_a, {"wide": partner})

            @pl.when(wraps & (z == 0))
            def _():
                pl.semaphore_wait(wrap_ok, 1)

            @pl.when(wrap_a & (z == 0))
            def _():
                tell(ready_a, {"narrow": n - 1})

            pass_on(ready_b, home_b)

            @pl.when(wrap_b & (z == 0))
            def _():
                tell(ready_b, {"narrow": n - 1})

        @pl.when(even & (z != home_a))
        def _():
            pl.semaphore_wait(ready_a, 1)

    pairs = (
        (vol_hbm, vol_ref), (rows_hbm, rows_ref), (places_hbm, places_ref),
        (k1_hbm, k1_ref), (k2_hbm, k2_ref), (cot_hbm, cot_ref),
    )
    copies = [pltpu.make_async_copy(source, target, loads.at[i]) for i, (source, target) in enumerate(pairs)]
    for copy in copies:
        copy.start()

    greeted = 2 * len(mates_near)
    for expected in (w > 0, w < n - 1, expects_above, expects_below, expects_first):
        greeted = greeted + jnp.where(expected, 1, 0)
    pl.semaphore_wait(barrier, greeted)
    meet(near1, mates_near)

    @pl.when(expects_first)
    def _():
        tell(wrap_ok, {"narrow": 0})

    @pl.when(odd & (z == home_a))
    def _():
        announce(ready_a, home_a)

    @pl.when(odd & (z == home_b))
    def _():
        announce(ready_b, home_b)

    source = lax.broadcasted_iota(jnp.int32, (512, 512), 0)
    target = lax.broadcasted_iota(jnp.int32, (512, 512), 1)
    goal = ((source // 64) % 2) * 256 + (source % 2) * 128 + (source // 128) * 32 + (source % 64) // 2
    lanes = jnp.where(goal == target, 1.0, 0.0).astype(BF16)
    for copy in copies[:2]:
        copy.wait()
    for ch in range(CIN):
        raw[4 * ch : 4 * ch + 4, :] = vol_ref[ch].astype(F32)
    blocks = [raw[:, 512 * j : 512 * j + 512].astype(BF16) for j in range(8)]
    spreadout = jnp.dot(jnp.concatenate(blocks, axis=0), lanes, preferred_element_type=F32).astype(BF16)
    joined = jnp.concatenate(
        [
            jnp.concatenate([spreadout[16 * j : 16 * j + 16, 128 * q : 128 * q + 128] for j in range(8)], axis=1)
            for q in range(4)
        ],
        axis=0,
    )
    planes[48:112, :] = jnp.dot(rows_ref[...], joined, preferred_element_type=F32).astype(BF16)

    @pl.when(first)
    def _():
        planes[0:48, :] = jnp.zeros((48, PLANE), BF16)

    @pl.when(last)
    def _():
        planes[112:144, :] = jnp.zeros((32, PLANE), BF16)

    upward = pltpu.make_async_remote_copy(
        planes.at[64:112], planes.at[0:48], halo_send.at[0], halo_recv.at[0],
        device_id={"wide": lax.rem(w + 1, n)}, device_id_type=MESH,
    )
    downward = pltpu.make_async_remote_copy(
        planes.at[48:80], planes.at[112:144], halo_send.at[1], halo_recv.at[1],
        device_id={"wide": lax.rem(w + n - 1, n)}, device_id_type=MESH,
    )

    @pl.when(jnp.logical_not(last))
    def _():
        upward.start()

    @pl.when(jnp.logical_not(first))
    def _():
        downward.start()

    met(near1, mates_near)
    meet(near2, mates_near)

    for copy in copies[2:]:
        copy.wait()
    for t in range(TAPS):
        stacked[CIN * t : CIN * t + CIN, :] = k1_ref[t].astype(F32)
    stacked[CIN * TAPS :, :] = jnp.zeros((128 - CIN * TAPS, C1), F32)
    placed = jnp.dot(places_ref[...], stacked[...].astype(BF16), preferred_element_type=F32).astype(BF16)
    weights1 = turned(placed, C1)[:, :192]
    for a in range(3):
        weights2[C2 * a : C2 * a + C2, :] = turned(k2_ref[9 * a : 9 * a + 9].reshape(ROWS2, C2), C2)

    lane = lax.broadcasted_iota(jnp.int32, (16, PLANE), 1)
    left_ok = (lane % HALF) != 0
    lower_ok = lane >= HALF

    def spread_plane(zi):
        base = planes[16 * zi : 16 * zi + 16, :].astype(F32)
        at_x = jnp.where(left_ok, rolled(base, 1), 0.0)
        at_y = jnp.where(lower_ok, rolled(base, HALF), 0.0)
        both = jnp.where(lower_ok, rolled(at_x, HALF), 0.0)
        for s, part in enumerate((base, at_x, at_y, both)):
            taps1[64 * zi + 16 * s : 64 * zi + 16 * s + 16, :] = part.astype(BF16)

    for zi in range(3, 7):
        spread_plane(zi)

    lane2 = lax.broadcasted_iota(jnp.int32, (C1, PLANE), 1)
    left2 = (lane2 % HALF) != 0
    right2 = (lane2 % HALF) != HALF - 1
    lower2 = lane2 >= HALF
    upper2 = lane2 < PLANE - HALF

    def first_layer(zo):
        pre = jnp.dot(weights1, taps1[128 * zo : 128 * zo + 192, :], preferred_element_type=F32)
        act = jnp.where(pre > 0, pre, SLOPE * pre)
        if zo == 3:
            act = jnp.where(last, 0.0, act)
        act = act.astype(BF16).astype(F32)
        shifted = (jnp.where(left2, rolled(act, 1), 0.0), act, jnp.where(right2, rolled(act, -1), 0.0))
        for c in range(3):
            parts = (
                jnp.where(lower2, rolled(shifted[c], HALF), 0.0),
                shifted[c],
                jnp.where(upper2, rolled(shifted[c], -HALF), 0.0),
            )
            for b in range(3):
                row = ROWS2 * zo + C1 * (3 * b + c)
                taps2[row : row + C1, :] = parts[b].astype(BF16)

    reached = [[a for a in range(3) if 0 <= zo - a <= 1] for zo in range(4)]

    def second_part(zo):
        low, count = reached[zo][0], len(reached[zo])
        parts2[zo, : C2 * count, :] = jnp.dot(
            weights2[C2 * low : C2 * (low + count), :], taps2[ROWS2 * zo : ROWS2 * zo + ROWS2, :],
            preferred_element_type=F32,
        )

    def second_sum(half):
        pre = None
        for a in range(3):
            at = C2 * reached[half + a].index(a)
            part = parts2[half + a, at : at + C2, :]
            pre = part if pre is None else pre + part
        cells = slice(PLANE * half, PLANE * half + PLANE)
        act_ref[:, cells] = jnp.where(pre > 0, pre, SLOPE * pre).astype(BF16)
        backs[half] = (cot_ref[:, cells].astype(F32) * jnp.where(pre > 0, 1.0, SLOPE)).astype(BF16)

    def gradient_part(zo):
        columns = jnp.concatenate(
            [backs[zo - a] if a in reached[zo] else jnp.zeros((C2, PLANE), BF16) for a in range(3)], axis=0
        )
        patches = taps2[ROWS2 * zo : ROWS2 * zo + ROWS2, :]
        return lax.dot_general(patches, columns, (((1,), (1,)), ((), ())), preferred_element_type=F32)

    first_layer(2)
    second_part(2)
    met(near2, mates_near)
    meet(near3, mates_near)

    @pl.when(jnp.logical_not(last))
    def _():
        upward.wait_send()
        downward.wait_recv()

    @pl.when(jnp.logical_not(first))
    def _():
        downward.wait_send()
        upward.wait_recv()

    for zi in (0, 1, 2, 7, 8):
        spread_plane(zi)
    for zo in (0, 1):
        first_layer(zo)
        second_part(zo)
    second_sum(0)
    first_layer(3)
    second_part(3)
    second_sum(1)
    total = gradient_part(0) + gradient_part(1) + gradient_part(2) + gradient_part(3)
    total = (total * scale).astype(BF16)
    total = jnp.concatenate([total[:, C2 * a : C2 * a + C2] for a in range(3)], axis=0)
    total = turned(total, C2, F32)
    met(near3, mates_near)

    for k in range(6):
        spread[pl.ds(k, C2, stride=8), :] = total[:, 128 * k : 128 * k + 128]
    rest = jnp.concatenate([total[:, 768:], jnp.zeros((C2, 896 - TAPS * C1), F32)], axis=1)
    spread[pl.ds(6, C2, stride=8), :] = rest
    spread[pl.ds(7, C2, stride=8), :] = jnp.zeros((C2, 128), F32)
    size = C2 // n * 8
    send1[...] = spread[...].astype(BF16).reshape(n, size, 128)
    recv1[w] = send1[w]

    far = [min(d, along - d) for d in range(along)], [min(d, across - d) for d in range(across)]
    offsets = [(dy, dx, dc) for dy in range(along) for dx in range(across) for dc in range(2)][1:]
    y_at = [lax.rem(y + d, along) * (2 * across) for d in range(along)]
    x_at = [lax.rem(x + d, across) * 2 for d in range(across)]
    core_at = [core, 1 - core]
    order = sorted(offsets, key=lambda d: -(2 * far[0][d[0]] + 2 * far[1][d[1]] + d[2]))
    mates = [y_at[dy] + x_at[dx] + core_at[dc] for dy, dx, dc in order]
    for to in mates:
        pltpu.make_async_remote_copy(
            send1.at[to], recv1.at[w], sem_send1, sem_recv1, device_id={"wide": to}, device_id_type=MESH
        ).start()
    relay()
    pltpu.make_async_copy(send1.at[pl.ds(0, n - 1)], send1.at[pl.ds(0, n - 1)], sem_send1).wait()
    pltpu.make_async_copy(recv1.at[pl.ds(0, n - 1)], recv1.at[pl.ds(0, n - 1)], sem_recv1).wait()

    send2[...] = jnp.sum(recv1[...].astype(F32), axis=0).astype(BF16)

    deliver = pltpu.make_async_remote_copy(
        send2, recv2.at[z], sem_send2, sem_recv2, device_id={"wide": home_b, "narrow": w}, device_id_type=MESH
    )

    @pl.when(jnp.logical_not(own_b))
    def _():
        deliver.start()
        deliver.wait_send()

    @pl.when(jnp.logical_not(owner))
    def _():
        pltpu.make_async_copy(final, final, sem_recv3).wait()

    @pl.when(own_a)
    def _():
        pltpu.make_async_copy(recv2, recv2, sem_recv2).wait()

    @pl.when(own_b)
    def _():
        recv2[z] = send2[...]
        pltpu.make_async_copy(recv2.at[pl.ds(0, n - 1)], recv2.at[pl.ds(0, n - 1)], sem_recv2).wait()

    @pl.when(owner)
    def _():
        whole = jnp.sum(recv2[...].astype(F32), axis=0).astype(BF16)
        send3[...] = whole
        final[...] = whole

        for to in mates:
            pltpu.make_async_remote_copy(
                send3, final, sem_send3, sem_recv3, device_id={"wide": to}, device_id_type=MESH
            ).start()

        pltpu.make_async_copy(recv2.at[pl.ds(0, n - 1)], recv2.at[pl.ds(0, n - 1)], sem_send3).wait()

    rows = C2 // n
    result = final[...].astype(F32)
    for t in range(TAPS):
        for r in range(rows):
            at = 8 * r + t // 4
            grad_ref[t, r : r + 1, :] = result[at : at + 1, C1 * (t % 4) : C1 * (t % 4) + C1]


def body(volumes, first_kernel, second_kernel, cotangent):
    n = lax.axis_size("wide")
    cells = cotangent.shape[3]
    scale = 1.0 / math.sqrt(n * lax.axis_size("narrow") * cells)
    size = C2 // n * 8
    vmem = pl.BlockSpec(memory_space=pltpu.VMEM)
    dma = pltpu.SemaphoreType.DMA
    inputs = (
        volumes.reshape(CIN, 4, 4096),
        jnp.asarray(row_order(), BF16),
        jnp.asarray(first_places(), BF16),
        first_kernel.transpose(0, 2, 1),
        second_kernel.transpose(0, 2, 1),
        cotangent.reshape(C2, cells),
    )
    act, grad = pl.pallas_call(
        functools.partial(kernel, n, scale),
        out_shape=(
            jax.ShapeDtypeStruct((C2, cells), BF16),
            jax.ShapeDtypeStruct((TAPS, C2 // n, C1), F32),
        ),
        in_specs=[pl.BlockSpec(memory_space=pltpu.HBM)] * len(inputs),
        out_specs=(vmem, vmem),
        scratch_shapes=[
            *[pltpu.VMEM(x.shape, BF16) for x in inputs],
            dma((len(inputs),)),
            pltpu.VMEM((16, 4096), F32),
            pltpu.VMEM((128, C1), F32),
            pltpu.VMEM((144, PLANE), BF16),
            pltpu.VMEM((576, PLANE), BF16),
            pltpu.VMEM((4 * ROWS2, PLANE), BF16),
            pltpu.VMEM((3 * C2, ROWS2), BF16),
            pltpu.VMEM((4, 2 * C2, PLANE), F32),
            pltpu.VMEM((2, C2, PLANE), BF16),
            pltpu.VMEM((C2 * 8, 128), F32),
            pltpu.VMEM((n, size, 128), BF16),
            pltpu.VMEM((n, size, 128), BF16),
            pltpu.VMEM((size, 128), BF16),
            pltpu.VMEM((n, size, 128), BF16),
            pltpu.VMEM((size, 128), BF16),
            pltpu.VMEM((size, 128), BF16),
            dma((2,)),
            dma((2,)),
            dma(()),
            dma(()),
            dma(()),
            dma(()),
            dma(()),
            dma(()),
            *[pltpu.SemaphoreType.REGULAR] * 6,
        ],
        compiler_params=pltpu.CompilerParams(collective_id=0, has_side_effects=True, vmem_limit_bytes=24 << 20),
    )(*[pltpu.with_memory_space_constraint(x, pltpu.HBM) for x in inputs])
    return act.reshape(1, 1, C2, cells), grad


def solution(mesh):
    return jax.shard_map(
        body,
        mesh=mesh,
        in_specs=(P("narrow", None, None, "wide", None), P(), P(), P("narrow", None, None, "wide")),
        out_specs=(P("narrow", None, None, "wide"), P(None, "narrow", None)),
        check_vma=False,
    )
```

```python
import functools
import math

import jax
import jax.numpy as jnp
import numpy as np
from jax import lax
from jax.experimental import pallas as pl
from jax.experimental.pallas import tpu as pltpu
from jax.sharding import PartitionSpec as P

CIN = 4
C1 = 32
C2 = 64
HALF = 32
PLANE = HALF * HALF
SLOPE = 0.3
TAPS = 27
ROWS2 = 9 * C1
F32 = jnp.float32
BF16 = jnp.bfloat16
MESH = pl.DeviceIdType.MESH


def row_order():
    order = np.zeros((64, 64), np.float32)
    for z in range(4):
        for q in range(4):
            for ch in range(CIN):
                order[z * 16 + q * 4 + ch, q * 16 + ch * 4 + z] = 1.0
    return order


def first_places():
    places = np.zeros((256, 128), np.float32)
    for t in range(TAPS):
        a, b, c = t // 9, t // 3 % 3, t % 3
        shift = (2 if b == 0 else 0) + (1 if c == 0 else 0)
        q = (0 if b == 1 else 2) + (0 if c == 1 else 1)
        for i in range(CIN):
            places[a * 64 + shift * 16 + q * 4 + i, CIN * t + i] = 1.0
    return places


def rolled(x, shift):
    return pltpu.roll(x, shift % PLANE, axis=1)


def turned(x, size, kind=BF16):
    rows = lax.broadcasted_iota(jnp.int32, (size, size), 0)
    columns = lax.broadcasted_iota(jnp.int32, (size, size), 1)
    same = jnp.where(rows == columns, 1.0, 0.0).astype(BF16)
    return lax.dot_general(same, x, (((1,), (1,)), ((), ())), preferred_element_type=F32).astype(kind)


def kernel(
    n, scale, vol_hbm, rows_hbm, places_hbm, k1_hbm, k2_hbm, cot_hbm,
    act_ref, grad_ref,
    vol_ref, rows_ref, places_ref, k1_ref, k2_ref, cot_ref, loads,
    raw, stacked, planes, taps1, taps2, weights2, parts2, backs, spread, send1, recv1, send2, recv2, send3, final,
    halo_send, halo_recv, sem_send1, sem_recv1, sem_send2, sem_recv2, sem_send3, sem_recv3,
    ready_a, ready_b, wrap_ok, near1, near2, near3,
):
    w = lax.axis_index("wide")
    z = lax.axis_index("narrow")
    core = lax.rem(w, 2)
    even, odd = core == 0, core == 1
    across = min(4, n // 2)
    along = n // 2 // across
    x = lax.rem(w // 2, across)
    y = w // (2 * across)
    partner = w + 1 - 2 * core
    row_mates = [(y * across + lax.rem(x + k, across)) * 2 + core for k in sorted({1, across - 1} - {0})]
    column_mates = [(lax.rem(y + k, along) * across + x) * 2 + core for k in sorted({1, along - 1} - {0}) if along > 1]
    first = w == 0
    last = w == n - 1
    barrier = pltpu.get_barrier_semaphore()

    def tell(semaphore, to):
        pl.semaphore_signal(semaphore, 1, device_id=to, device_id_type=MESH)

    @pl.when(jnp.logical_not(first))
    def _():
        tell(barrier, {"wide": w - 1})

    @pl.when(jnp.logical_not(last))
    def _():
        tell(barrier, {"wide": w + 1})

    mates_near = row_mates + column_mates
    for mate in mates_near:
        tell(barrier, {"wide": mate})
        tell(barrier, {"wide": mate + 1 - 2 * core})

    home_a = w - core
    home_b = w - core + 1
    own_a, own_b = odd & (z == home_a), odd & (z == home_b)
    owner = own_a | own_b

    turn = min(n - 1, 3 * n // 4 + 1)

    def forwards(at, home):
        gap = lax.rem(at - home + 2 * n, n)
        reach = jnp.where(home > n // 2, n // 2, jnp.where(home == n // 2, n - 1, turn) - home)
        return gap < reach, jnp.where(gap == 0, reach < n - 1, gap > reach + 1)

    def sides(at):
        up_a, down_a = forwards(at, home_a)
        up_b, down_b = forwards(at, home_b)
        return odd & (up_a | up_b), odd & (down_a | down_b) & (at != 0)

    above = lax.rem(z + 1, n)
    below = lax.rem(z + n - 1, n)

    @pl.when(sides(below)[0])
    def _():
        tell(barrier, {"narrow": below})

    @pl.when(sides(above)[1])
    def _():
        tell(barrier, {"narrow": above})

    expects_above, expects_below = sides(z)

    wrap_a, wrap_b = forwards(0, home_a)[1], forwards(0, home_b)[1]
    wraps = odd & (wrap_a | wrap_b)

    @pl.when(wraps & (z == 0))
    def _():
        tell(barrier, {"narrow": n - 1})

    expects_first = wraps & (z == n - 1)

    def meet(semaphore, mates):
        for mate in mates:
            tell(semaphore, {"wide": mate})

    def met(semaphore, mates):
        if mates:
            pl.semaphore_wait(semaphore, len(mates))

    def announce(semaphore, home):
        up, down = forwards(z, home)

        @pl.when(up)
        def _():
            tell(semaphore, {"narrow": above})

        @pl.when(down & (z > 0))
        def _():
            tell(semaphore, {"narrow": below})

    def pass_on(semaphore, home):
        @pl.when(z != home)
        def _():
            pl.semaphore_wait(semaphore, 1)
            announce(semaphore, home)

    def relay():
        @pl.when(odd)
        def _():
            pass_on(ready_a, home_a)

            @pl.when(z != home_a)
            def _():
                tell(ready_a, {"wide": partner})

            @pl.when(wraps & (z == 0))
            def _():
                pl.semaphore_wait(wrap_ok, 1)

            @pl.when(wrap_a & (z == 0))
            def _():
                tell(ready_a, {"narrow": n - 1})

            pass_on(ready_b, home_b)

            @pl.when(wrap_b & (z == 0))
            def _():
                tell(ready_b, {"narrow": n - 1})

        @pl.when(even & (z != home_a))
        def _():
            pl.semaphore_wait(ready_a, 1)

    pairs = (
        (vol_hbm, vol_ref), (rows_hbm, rows_ref), (places_hbm, places_ref),
        (k1_hbm, k1_ref), (k2_hbm, k2_ref), (cot_hbm, cot_ref),
    )
    copies = [pltpu.make_async_copy(source, target, loads.at[i]) for i, (source, target) in enumerate(pairs)]
    for copy in copies:
        copy.start()

    greeted = 2 * len(mates_near)
    for expected in (w > 0, w < n - 1, expects_above, expects_below, expects_first):
        greeted = greeted + jnp.where(expected, 1, 0)
    pl.semaphore_wait(barrier, greeted)
    meet(near1, mates_near)

    @pl.when(expects_first)
    def _():
        tell(wrap_ok, {"narrow": 0})

    @pl.when(odd & (z == home_a))
    def _():
        announce(ready_a, home_a)

    @pl.when(odd & (z == home_b))
    def _():
        announce(ready_b, home_b)

    source = lax.broadcasted_iota(jnp.int32, (512, 512), 0)
    target = lax.broadcasted_iota(jnp.int32, (512, 512), 1)
    goal = ((source // 64) % 2) * 256 + (source % 2) * 128 + (source // 128) * 32 + (source % 64) // 2
    lanes = jnp.where(goal == target, 1.0, 0.0).astype(BF16)
    for copy in copies[:2]:
        copy.wait()
    for ch in range(CIN):
        raw[4 * ch : 4 * ch + 4, :] = vol_ref[ch].astype(F32)
    blocks = [raw[:, 512 * j : 512 * j + 512].astype(BF16) for j in range(8)]
    spreadout = jnp.dot(jnp.concatenate(blocks, axis=0), lanes, preferred_element_type=F32).astype(BF16)
    joined = jnp.concatenate(
        [
            jnp.concatenate([spreadout[16 * j : 16 * j + 16, 128 * q : 128 * q + 128] for j in range(8)], axis=1)
            for q in range(4)
        ],
        axis=0,
    )
    planes[48:112, :] = jnp.dot(rows_ref[...], joined, preferred_element_type=F32).astype(BF16)

    @pl.when(first)
    def _():
        planes[0:48, :] = jnp.zeros((48, PLANE), BF16)

    @pl.when(last)
    def _():
        planes[112:144, :] = jnp.zeros((32, PLANE), BF16)

    upward = pltpu.make_async_remote_copy(
        planes.at[64:112], planes.at[0:48], halo_send.at[0], halo_recv.at[0],
        device_id={"wide": lax.rem(w + 1, n)}, device_id_type=MESH,
    )
    downward = pltpu.make_async_remote_copy(
        planes.at[48:80], planes.at[112:144], halo_send.at[1], halo_recv.at[1],
        device_id={"wide": lax.rem(w + n - 1, n)}, device_id_type=MESH,
    )

    @pl.when(jnp.logical_not(last))
    def _():
        upward.start()

    @pl.when(jnp.logical_not(first))
    def _():
        downward.start()

    met(near1, mates_near)
    meet(near2, mates_near)

    for copy in copies[2:]:
        copy.wait()
    for t in range(TAPS):
        stacked[CIN * t : CIN * t + CIN, :] = k1_ref[t].astype(F32)
    stacked[CIN * TAPS :, :] = jnp.zeros((128 - CIN * TAPS, C1), F32)
    placed = jnp.dot(places_ref[...], stacked[...].astype(BF16), preferred_element_type=F32).astype(BF16)
    weights1 = turned(placed, C1)[:, :192]
    for a in range(3):
        weights2[C2 * a : C2 * a + C2, :] = turned(k2_ref[9 * a : 9 * a + 9].reshape(ROWS2, C2), C2)

    lane = lax.broadcasted_iota(jnp.int32, (16, PLANE), 1)
    left_ok = (lane % HALF) != 0
    lower_ok = lane >= HALF

    def spread_plane(zi):
        base = planes[16 * zi : 16 * zi + 16, :].astype(F32)
        at_x = jnp.where(left_ok, rolled(base, 1), 0.0)
        at_y = jnp.where(lower_ok, rolled(base, HALF), 0.0)
        both = jnp.where(lower_ok, rolled(at_x, HALF), 0.0)
        for s, part in enumerate((base, at_x, at_y, both)):
            taps1[64 * zi + 16 * s : 64 * zi + 16 * s + 16, :] = part.astype(BF16)

    for zi in range(3, 7):
        spread_plane(zi)

    lane2 = lax.broadcasted_iota(jnp.int32, (C1, PLANE), 1)
    left2 = (lane2 % HALF) != 0
    right2 = (lane2 % HALF) != HALF - 1
    lower2 = lane2 >= HALF
    upper2 = lane2 < PLANE - HALF

    def first_layer(zo):
        pre = jnp.dot(weights1, taps1[128 * zo : 128 * zo + 192, :], preferred_element_type=F32)
        act = jnp.where(pre > 0, pre, SLOPE * pre)
        if zo == 3:
            act = jnp.where(last, 0.0, act)
        act = act.astype(BF16).astype(F32)
        shifted = (jnp.where(left2, rolled(act, 1), 0.0), act, jnp.where(right2, rolled(act, -1), 0.0))
        for c in range(3):
            parts = (
                jnp.where(lower2, rolled(shifted[c], HALF), 0.0),
                shifted[c],
                jnp.where(upper2, rolled(shifted[c], -HALF), 0.0),
            )
            for b in range(3):
                row = ROWS2 * zo + C1 * (3 * b + c)
                taps2[row : row + C1, :] = parts[b].astype(BF16)

    reached = [[a for a in range(3) if 0 <= zo - a <= 1] for zo in range(4)]

    def second_part(zo):
        low, count = reached[zo][0], len(reached[zo])
        parts2[zo, : C2 * count, :] = jnp.dot(
            weights2[C2 * low : C2 * (low + count), :], taps2[ROWS2 * zo : ROWS2 * zo + ROWS2, :],
            preferred_element_type=F32,
        )

    def second_pre(half):
        pre = None
        for a in range(3):
            at = C2 * reached[half + a].index(a)
            part = parts2[half + a, at : at + C2, :]
            pre = part if pre is None else pre + part
        return pre

    def second_act(half):
        pre = second_pre(half)
        cells = slice(PLANE * half, PLANE * half + PLANE)
        act_ref[:, cells] = jnp.where(pre > 0, pre, SLOPE * pre).astype(BF16)

    def second_sum(half):
        pre = second_pre(half)
        cells = slice(PLANE * half, PLANE * half + PLANE)
        backs[half] = (cot_ref[:, cells].astype(F32) * jnp.where(pre > 0, 1.0, SLOPE)).astype(BF16)

    def gradient_part(zo):
        columns = jnp.concatenate(
            [backs[zo - a] if a in reached[zo] else jnp.zeros((C2, PLANE), BF16) for a in range(3)], axis=0
        )
        patches = taps2[ROWS2 * zo : ROWS2 * zo + ROWS2, :]
        return lax.dot_general(patches, columns, (((1,), (1,)), ((), ())), preferred_element_type=F32)

    first_layer(2)
    second_part(2)
    met(near2, mates_near)
    meet(near3, mates_near)

    @pl.when(jnp.logical_not(last))
    def _():
        upward.wait_send()
        downward.wait_recv()

    @pl.when(jnp.logical_not(first))
    def _():
        downward.wait_send()
        upward.wait_recv()

    for zi in (0, 1, 2, 7, 8):
        spread_plane(zi)
    for zo in (0, 1):
        first_layer(zo)
        second_part(zo)
    second_sum(0)
    first_layer(3)
    second_part(3)
    second_sum(1)
    total = gradient_part(0) + gradient_part(1) + gradient_part(2) + gradient_part(3)
    total = (total * scale).astype(BF16)
    total = jnp.concatenate([total[:, C2 * a : C2 * a + C2] for a in range(3)], axis=0)
    total = turned(total, C2, F32)
    met(near3, mates_near)

    for k in range(6):
        spread[pl.ds(k, C2, stride=8), :] = total[:, 128 * k : 128 * k + 128]
    rest = jnp.concatenate([total[:, 768:], jnp.zeros((C2, 896 - TAPS * C1), F32)], axis=1)
    spread[pl.ds(6, C2, stride=8), :] = rest
    spread[pl.ds(7, C2, stride=8), :] = jnp.zeros((C2, 128), F32)
    size = C2 // n * 8
    send1[...] = spread[...].astype(BF16).reshape(n, size, 128)
    recv1[w] = send1[w]

    far = [min(d, along - d) for d in range(along)], [min(d, across - d) for d in range(across)]
    offsets = [(dy, dx, dc) for dy in range(along) for dx in range(across) for dc in range(2)][1:]
    y_at = [lax.rem(y + d, along) * (2 * across) for d in range(along)]
    x_at = [lax.rem(x + d, across) * 2 for d in range(across)]
    core_at = [core, 1 - core]
    order = sorted(offsets, key=lambda d: -(2 * far[0][d[0]] + 2 * far[1][d[1]] + d[2]))
    mates = [y_at[dy] + x_at[dx] + core_at[dc] for dy, dx, dc in order]
    for to in mates:
        pltpu.make_async_remote_copy(
            send1.at[to], recv1.at[w], sem_send1, sem_recv1, device_id={"wide": to}, device_id_type=MESH
        ).start()
    relay()
    second_act(0)
    second_act(1)
    pltpu.make_async_copy(send1.at[pl.ds(0, n - 1)], send1.at[pl.ds(0, n - 1)], sem_send1).wait()
    pltpu.make_async_copy(recv1.at[pl.ds(0, n - 1)], recv1.at[pl.ds(0, n - 1)], sem_recv1).wait()

    send2[...] = jnp.sum(recv1[...].astype(F32), axis=0).astype(BF16)

    deliver = pltpu.make_async_remote_copy(
        send2, recv2.at[z], sem_send2, sem_recv2, device_id={"wide": home_b, "narrow": w}, device_id_type=MESH
    )

    @pl.when(jnp.logical_not(own_b))
    def _():
        deliver.start()
        deliver.wait_send()

    @pl.when(jnp.logical_not(owner))
    def _():
        pltpu.make_async_copy(final, final, sem_recv3).wait()

    @pl.when(own_a)
    def _():
        pltpu.make_async_copy(recv2, recv2, sem_recv2).wait()

    @pl.when(own_b)
    def _():
        recv2[z] = send2[...]
        pltpu.make_async_copy(recv2.at[pl.ds(0, n - 1)], recv2.at[pl.ds(0, n - 1)], sem_recv2).wait()

    @pl.when(owner)
    def _():
        whole = jnp.sum(recv2[...].astype(F32), axis=0).astype(BF16)
        send3[...] = whole
        final[...] = whole

        for to in mates:
            pltpu.make_async_remote_copy(
                send3, final, sem_send3, sem_recv3, device_id={"wide": to}, device_id_type=MESH
            ).start()

        pltpu.make_async_copy(recv2.at[pl.ds(0, n - 1)], recv2.at[pl.ds(0, n - 1)], sem_send3).wait()

    rows = C2 // n
    result = final[...].astype(F32)
    for t in range(TAPS):
        for r in range(rows):
            at = 8 * r + t // 4
            grad_ref[t, r : r + 1, :] = result[at : at + 1, C1 * (t % 4) : C1 * (t % 4) + C1]


def body(volumes, first_kernel, second_kernel, cotangent):
    n = lax.axis_size("wide")
    cells = cotangent.shape[3]
    scale = 1.0 / math.sqrt(n * lax.axis_size("narrow") * cells)
    size = C2 // n * 8
    vmem = pl.BlockSpec(memory_space=pltpu.VMEM)
    dma = pltpu.SemaphoreType.DMA
    inputs = (
        volumes.reshape(CIN, 4, 4096),
        jnp.asarray(row_order(), BF16),
        jnp.asarray(first_places(), BF16),
        first_kernel.transpose(0, 2, 1),
        second_kernel.transpose(0, 2, 1),
        cotangent.reshape(C2, cells),
    )
    act, grad = pl.pallas_call(
        functools.partial(kernel, n, scale),
        out_shape=(
            jax.ShapeDtypeStruct((C2, cells), BF16),
            jax.ShapeDtypeStruct((TAPS, C2 // n, C1), F32),
        ),
        in_specs=[pl.BlockSpec(memory_space=pltpu.HBM)] * len(inputs),
        out_specs=(vmem, vmem),
        scratch_shapes=[
            *[pltpu.VMEM(x.shape, BF16) for x in inputs],
            dma((len(inputs),)),
            pltpu.VMEM((16, 4096), F32),
            pltpu.VMEM((128, C1), F32),
            pltpu.VMEM((144, PLANE), BF16),
            pltpu.VMEM((576, PLANE), BF16),
            pltpu.VMEM((4 * ROWS2, PLANE), BF16),
            pltpu.VMEM((3 * C2, ROWS2), BF16),
            pltpu.VMEM((4, 2 * C2, PLANE), F32),
            pltpu.VMEM((2, C2, PLANE), BF16),
            pltpu.VMEM((C2 * 8, 128), F32),
            pltpu.VMEM((n, size, 128), BF16),
            pltpu.VMEM((n, size, 128), BF16),
            pltpu.VMEM((size, 128), BF16),
            pltpu.VMEM((n, size, 128), BF16),
            pltpu.VMEM((size, 128), BF16),
            pltpu.VMEM((size, 128), BF16),
            dma((2,)),
            dma((2,)),
            dma(()),
            dma(()),
            dma(()),
            dma(()),
            dma(()),
            dma(()),
            *[pltpu.SemaphoreType.REGULAR] * 6,
        ],
        compiler_params=pltpu.CompilerParams(collective_id=0, has_side_effects=True, vmem_limit_bytes=24 << 20),
    )(*[pltpu.with_memory_space_constraint(x, pltpu.HBM) for x in inputs])
    return act.reshape(1, 1, C2, cells), grad


def solution(mesh):
    return jax.shard_map(
        body,
        mesh=mesh,
        in_specs=(P("narrow", None, None, "wide", None), P(), P(), P("narrow", None, None, "wide")),
        out_specs=(P("narrow", None, None, "wide"), P(None, "narrow", None)),
        check_vma=False,
    )
```
